32 devices in a mesh: member: 2 (over y), lon: 4 (over z), lat: 2 (over x), dp: 2 (over core).
Axes of the slice: x: 2, y: 2, z: 4, core: 2. Of those that a mesh axis runs over, the one named last changes fastest.
Arguments:
- fields: bfloat16 [4, 64, 32, 512], P(('member', 'dp'), 'lat', 'lon'), parts along dimension 0, may hold values from -6 to 6
- cotangent: bfloat16 [4, 64, 32, 512], P(('member', 'dp'), 'lat', 'lon'), parts along dimension 0, may hold values from -6 to 6
- conv_weight: float32 [7, 7, 512], replicated, may hold values from -0.875 to 0.875
- norm_gain: float32 [512], replicated, may hold values from 0.1 to 1.9
- w_qkv: bfloat16 [512, 768], replicated, may hold values from -1 to 1
- w_out: bfloat16 [256, 512], replicated, may hold values from -0.375 to 0.375
Outputs:
- result: bfloat16 [4, 64, 32, 512], P(('member', 'dp'), 'lat', 'lon'), parts along dimension 0
- grad_fields: bfloat16 [4, 64, 32, 512], P(('member', 'dp'), 'lat', 'lon'), parts along dimension 0
- grad_qkv: float32 [1024, 768], P('member'), parts along dimension 0
- grad_out: float32 [512, 512], P('member'), parts along dimension 0
- grad_conv: float32 [14, 7, 512], P('member'), parts along dimension 0
- grad_gain: float32 [1024], P('member'), parts along dimension 0
The draws below stay inside these ranges and needn't reach their ends.
There are 2 independent parts, one for each index of `member`. The reference program is written for one: setup_inputs(seed, part) draws one part's arguments, and reference() takes and returns one part's arrays. A program takes and returns all parts, laid end to end along the dimension named above; an argument that names none is the same for every part. Nothing has to cross between parts.
All inputs are finite; a program needn't handle non-finite values.
Results may differ from the reference program's by a relative error of at most 0.012.
The reference program's roundings to bfloat16 on the way (of `normed`, `projected`, `weights`, `mixed`, `grad_mixed`, `grad_scores` and `grad_projected`) count: a program that leaves them out, or rounds other values in their place, can miss the bound.
Values may be sent and summed in bfloat16 or wider, within the bound.
A program may use at most 64 MiB of HBM per device.

```python
import jax
import jax.numpy as jnp
from jax import lax

D = 512
HEADS = 4
HEAD_DIM = 64
ATT_WIDTH = 256
BATCH = 2
LAT = 64
LON = 32


def draw_w_qkv(key, part):
    base_key = jax.random.fold_in(key, 0)
    deviation = (D // 3) ** (-0.5)
    drawn = jax.random.normal(base_key, (D, 3 * ATT_WIDTH), jnp.float32) * deviation
    drawn = jnp.clip(drawn, -4.0 * deviation, 4.0 * deviation)
    return drawn.astype(jnp.bfloat16)


def steps_of(own_key, shape, cuts, smallest, top_value):
    loudness = 1.0
    for position, shards_of in cuts:
        heights = jax.random.uniform(jax.random.fold_in(jax.random.fold_in(own_key, 6), position), (shards_of,), jnp.float32, smallest / len(cuts), top_value / len(cuts))
        loudness = loudness * jnp.repeat(jnp.exp(heights), shape[position] // shards_of).reshape((-1,) + (1,) * (len(shape) - 1 - position))
    return loudness


def bell_draw(own_key, extent, scale, bound, cuts=(), kind=jnp.bfloat16):
    factor_of = steps_of(own_key, extent, cuts, -0.22, 0.18) if cuts else 1.0
    drawn = jax.random.normal(own_key, extent, jnp.float32) * scale * factor_of
    return jnp.minimum(jnp.maximum(drawn, -bound), bound).astype(kind)


def setup_inputs(seed: int = 0, part: int = 0) -> dict:
    streams_of = jax.random.split(jax.random.key(seed), 7)
    part_keys = jax.random.split(jax.random.fold_in(streams_of[6], part), 7)
    return {
        "fields": bell_draw(part_keys[0], (BATCH, LAT, LON, D), 1.0, 6.0, ((0, 2), (1, 2), (2, 4))),
        "cotangent": bell_draw(part_keys[1], (BATCH, LAT, LON, D), 1.0, 6.0, ((0, 2), (1, 2), (2, 4))),
        "conv_weight": bell_draw(streams_of[2], (7, 7, D), 49 ** -0.5, 0.875, (), jnp.float32),
        "norm_gain": jnp.clip(1.0 + 0.18 * jax.random.normal(streams_of[3], (D,), jnp.float32), 0.1, 1.9),
        "w_qkv": draw_w_qkv(jax.random.fold_in(streams_of[6], 71), part),
        "w_out": bell_draw(streams_of[5], (ATT_WIDTH, D), ATT_WIDTH ** -0.5, 0.375),
    }


EPSILON = 1e-06

def wrap_pad(values):
    padded = jnp.pad(values, ((3, 3), (0, 0), (0, 0)))
    return jnp.concatenate([padded[:, -3:], padded, padded[:, :3]], axis=1)

def spread(padded, kernel, lat_rows, lon_cols):
    summed = jnp.zeros((lat_rows, lon_cols, padded.shape[2]), jnp.float32)
    for row_shift in range(7):
        for col_shift in range(7):
            window = padded[row_shift:row_shift + lat_rows, col_shift:col_shift + lon_cols]
            summed = summed + kernel[row_shift, col_shift] * window
    return summed

def correlate(padded, upstream, lat_rows, lon_cols):
    pieces = []
    for row_shift in range(7):
        for col_shift in range(7):
            window = padded[row_shift:row_shift + lat_rows, col_shift:col_shift + lon_cols]
            pieces.append(lax.optimization_barrier(jnp.sum(window * upstream, axis=(0, 1))))
    return jnp.stack(pieces).reshape(7, 7, -1)

def split_heads(values):
    return values.reshape(values.shape[:-1] + (HEADS, HEAD_DIM)).astype(jnp.float32)

def attend_forward(projected):
    queries = split_heads(projected[..., :ATT_WIDTH])
    keys_part = split_heads(projected[..., ATT_WIDTH:2 * ATT_WIDTH])
    values_part = split_heads(projected[..., 2 * ATT_WIDTH:])
    scores = jnp.einsum('...qhd,...khd->...hqk', queries, keys_part) * HEAD_DIM ** (-0.5)
    probs = jax.nn.softmax(scores, axis=-1)
    weights = lax.optimization_barrier(probs.astype(jnp.bfloat16)).astype(jnp.float32)
    mixed = jnp.einsum('...hqk,...khd->...qhd', weights, values_part)
    return (mixed.reshape(projected.shape[:-1] + (ATT_WIDTH,)).astype(jnp.bfloat16), probs)

def attend_backward(projected, probs, grad_mixed):
    queries = split_heads(projected[..., :ATT_WIDTH])
    keys_part = split_heads(projected[..., ATT_WIDTH:2 * ATT_WIDTH])
    values_part = split_heads(projected[..., 2 * ATT_WIDTH:])
    grad_heads = split_heads(grad_mixed)
    weights = lax.optimization_barrier(probs.astype(jnp.bfloat16)).astype(jnp.float32)
    grad_probs = jnp.einsum('...qhd,...khd->...hqk', grad_heads, values_part)
    inner = lax.optimization_barrier(jnp.sum(probs * grad_probs, -1, keepdims=True))
    grad_scores = (probs * (grad_probs - inner) * HEAD_DIM ** (-0.5)).astype(jnp.bfloat16)
    grad_scores = lax.optimization_barrier(grad_scores).astype(jnp.float32)
    grad_query = jnp.einsum('...hqk,...khd->...qhd', grad_scores, keys_part)
    grad_key = jnp.einsum('...hqk,...qhd->...khd', grad_scores, queries)
    grad_value = jnp.einsum('...hqk,...qhd->...khd', weights, grad_heads)
    shaped = projected.shape[:-1] + (ATT_WIDTH,)
    return jnp.concatenate([grad_query.reshape(shaped).astype(jnp.bfloat16), grad_key.reshape(shaped).astype(jnp.bfloat16), grad_value.reshape(shaped).astype(jnp.bfloat16)], axis=-1)

def reference(fields, cotangent, conv_weight, norm_gain, w_qkv, w_out):

    def single_sample(paired):
        sample, upstream = paired
        sample_float = sample.astype(jnp.float32)
        padded = wrap_pad(sample_float)
        update = sample_float + spread(padded, conv_weight, LAT, LON)
        inverse = lax.rsqrt(lax.optimization_barrier(jnp.mean(update * update, -1, keepdims=True)) + EPSILON)
        normed = (update * inverse * norm_gain).astype(jnp.bfloat16)
        normed_flat = normed.reshape(LAT * LON, D)
        projected = jnp.dot(normed_flat, w_qkv, preferred_element_type=jnp.float32).astype(jnp.bfloat16)
        projected = projected.reshape(LAT, LON, 3 * ATT_WIDTH)
        mixed, probs = attend_forward(projected)
        mixed_flat = mixed.reshape(LAT * LON, ATT_WIDTH)
        result = (update + jnp.dot(mixed_flat, w_out, preferred_element_type=jnp.float32).reshape(LAT, LON, D)).astype(jnp.bfloat16)
        upstream_flat = upstream.reshape(LAT * LON, D)
        grad_mixed = jnp.dot(upstream_flat, w_out.T, preferred_element_type=jnp.float32).astype(jnp.bfloat16)
        grad_out = jnp.dot(mixed_flat.T, upstream_flat, preferred_element_type=jnp.float32)
        grad_projected = attend_backward(projected, probs, grad_mixed.reshape(LAT, LON, ATT_WIDTH))
        grad_flat = grad_projected.reshape(LAT * LON, 3 * ATT_WIDTH)
        grad_weight = jnp.dot(normed_flat.T, grad_flat, preferred_element_type=jnp.float32)
        grad_normed = jnp.dot(grad_flat, w_qkv.T, preferred_element_type=jnp.float32).reshape(LAT, LON, D)
        grad_gain = lax.optimization_barrier(jnp.sum(grad_normed * (update * inverse), axis=(0, 1)))
        gained = norm_gain * grad_normed
        grad_update = upstream.astype(jnp.float32) + inverse * gained - update * inverse ** 3 * lax.optimization_barrier(jnp.mean(gained * update, -1, keepdims=True))
        grad_sample = (grad_update + spread(wrap_pad(grad_update), conv_weight[::-1, ::-1], LAT, LON)).astype(jnp.bfloat16)
        grad_conv = correlate(padded, grad_update, LAT, LON)
        return (result, grad_sample, grad_weight, grad_out, grad_conv, grad_gain)
    outputs = lax.map(single_sample, (fields, cotangent))
    return (outputs[0], outputs[1], lax.optimization_barrier(jnp.sum(outputs[2], 0)), lax.optimization_barrier(jnp.sum(outputs[3], 0)), lax.optimization_barrier(jnp.sum(outputs[4], 0)), lax.optimization_barrier(jnp.sum(outputs[5], 0)))
```

```python
import functools
import itertools

import jax
import jax.numpy as jnp
from jax import lax
from jax.experimental import pallas as pl
from jax.experimental.pallas import tpu as pltpu
from jax.sharding import PartitionSpec as P

HEADS = 4
HEAD_DIM = 64


EPSILON = 1e-06


def with_halo(x, sides, width, wrap):
    for axis, dim in sides:
        size, length = (lax.axis_size(axis), x.shape[dim])
        up = [(i, (i + 1) % size) for i in range(size if wrap else size - 1)]
        down = [(j, i) for i, j in up]
        last = lax.slice_in_dim(x, length - width, length, axis=dim)
        first = lax.slice_in_dim(x, 0, width, axis=dim)
        before = lax.ppermute(last, axis, up)
        after = lax.ppermute(first, axis, down)
        x = jnp.concatenate([before, x, after], axis=dim)
    return x


def spread(padded, kernel, lat_rows, lon_cols):
    summed = jnp.zeros(padded.shape[:1] + (lat_rows, lon_cols, padded.shape[3]), jnp.float32)
    for row_shift in range(7):
        band = padded[:, row_shift : row_shift + lat_rows].astype(jnp.float32)
        partial_row = kernel[row_shift, 0] * band[:, :, 0:lon_cols]
        for col_shift in range(1, 7):
            partial_row = (
                partial_row
                + kernel[row_shift, col_shift] * band[:, :, col_shift : col_shift + lon_cols]
            )
        summed = summed + partial_row
    return summed


def correlate(padded, upstream, lat_rows, lon_cols):
    pieces = []
    for row_shift in range(7):
        for col_shift in range(7):
            window = padded[
                :, row_shift : row_shift + lat_rows, col_shift : col_shift + lon_cols
            ].astype(jnp.float32)
            pieces.append(jnp.sum(window * upstream, axis=(0, 1, 2)))
    return jnp.stack(pieces).reshape(7, 7, -1)


def split_heads(values):
    return values.reshape(values.shape[:-1] + (HEADS, HEAD_DIM))


def attend_forward(rowwise, att_width):
    queries = split_heads(rowwise[..., :att_width])
    keys_part = split_heads(rowwise[..., att_width : 2 * att_width])
    values_part = split_heads(rowwise[..., 2 * att_width :])
    scores = jnp.einsum(
        "brqhd,brkhd->brhqk", queries, keys_part, preferred_element_type=jnp.float32
    ) * HEAD_DIM ** (-0.5)
    row_peak = jnp.max(scores, -1, keepdims=True)
    raised = jnp.exp(scores - row_peak)
    probs = raised / jnp.sum(raised, -1, keepdims=True)
    weights = probs.astype(jnp.bfloat16)
    mixed = jnp.einsum(
        "brhqk,brkhd->brqhd", weights, values_part, preferred_element_type=jnp.float32
    )
    return (mixed.reshape(rowwise.shape[:3] + (att_width,)).astype(jnp.bfloat16), probs)


def attend_backward(rowwise, probs, grad_rowwise, att_width):
    queries = split_heads(rowwise[..., :att_width])
    keys_part = split_heads(rowwise[..., att_width : 2 * att_width])
    values_part = split_heads(rowwise[..., 2 * att_width :])
    grad_heads = split_heads(grad_rowwise)
    weights = probs.astype(jnp.bfloat16)
    grad_probs = jnp.einsum(
        "brqhd,brkhd->brhqk", grad_heads, values_part, preferred_element_type=jnp.float32
    )
    inner = jnp.sum(probs * grad_probs, -1, keepdims=True)
    grad_scores = (probs * (grad_probs - inner) * HEAD_DIM ** (-0.5)).astype(jnp.bfloat16)
    grad_query = jnp.einsum(
        "brhqk,brkhd->brqhd", grad_scores, keys_part, preferred_element_type=jnp.float32
    )
    grad_key = jnp.einsum(
        "brhqk,brqhd->brkhd", grad_scores, queries, preferred_element_type=jnp.float32
    )
    grad_value = jnp.einsum(
        "brhqk,brqhd->brkhd", weights, grad_heads, preferred_element_type=jnp.float32
    )
    shaped = rowwise.shape[:3] + (att_width,)
    return jnp.concatenate(
        [
            grad_query.reshape(shaped).astype(jnp.bfloat16),
            grad_key.reshape(shaped).astype(jnp.bfloat16),
            grad_value.reshape(shaped).astype(jnp.bfloat16),
        ],
        axis=-1,
    )


def contract_rows(left, right):
    return lax.dot_general(
        left, right, (((0,), (0,)), ((), ())), preferred_element_type=jnp.float32
    )


def contract_cols(left, right):
    return lax.dot_general(
        left, right, (((1,), (1,)), ((), ())), preferred_element_type=jnp.float32
    )


def on_device_native(fields, cotangent, conv_weight, norm_gain, w_qkv, w_out):
    batch_count, lat_rows, lon_cols, channels = fields.shape
    att_width = w_out.shape[0]
    wide = with_halo(fields, (("lon", 2),), 3, True)
    padded = with_halo(wide, (("lat", 1),), 3, False)
    update = fields.astype(jnp.float32) + spread(padded, conv_weight, lat_rows, lon_cols)
    inverse = lax.rsqrt(jnp.mean(update * update, -1, keepdims=True) + EPSILON)
    normed = (update * inverse * norm_gain).astype(jnp.bfloat16)
    normed_flat = normed.reshape(-1, channels)
    projected = jnp.dot(normed_flat, w_qkv, preferred_element_type=jnp.float32).astype(jnp.bfloat16)
    rowwise = lax.all_to_all(
        projected.reshape(batch_count, lat_rows, lon_cols, 3 * att_width),
        "lon",
        split_axis=1,
        concat_axis=2,
        tiled=True,
    )
    mixed_rows, probs = attend_forward(rowwise, att_width)
    mixed = lax.all_to_all(mixed_rows, "lon", split_axis=2, concat_axis=1, tiled=True)
    mixed_flat = mixed.reshape(-1, att_width)
    result = (
        update
        + jnp.dot(mixed_flat, w_out, preferred_element_type=jnp.float32).reshape(update.shape)
    ).astype(jnp.bfloat16)
    upstream_flat = cotangent.reshape(-1, channels)
    grad_mixed = contract_cols(upstream_flat, w_out).astype(jnp.bfloat16)
    grad_out = contract_rows(mixed_flat, upstream_flat)
    grad_rowwise = lax.all_to_all(
        grad_mixed.reshape(batch_count, lat_rows, lon_cols, att_width),
        "lon",
        split_axis=1,
        concat_axis=2,
        tiled=True,
    )
    grad_projected_rows = attend_backward(rowwise, probs, grad_rowwise, att_width)
    grad_projected = lax.all_to_all(
        grad_projected_rows, "lon", split_axis=2, concat_axis=1, tiled=True
    )
    grad_flat = grad_projected.reshape(-1, 3 * att_width)
    grad_weight = contract_rows(normed_flat, grad_flat)
    grad_normed = contract_cols(grad_flat, w_qkv).reshape(update.shape)
    grad_gain = jnp.sum(grad_normed * (update * inverse), axis=(0, 1, 2))
    gained = norm_gain * grad_normed
    grad_update = (
        cotangent.astype(jnp.float32)
        + inverse * gained
        - update * inverse**3 * jnp.mean(gained * update, -1, keepdims=True)
    )
    grad_wide = with_halo(grad_update.astype(jnp.bfloat16), (("lon", 2),), 3, True).astype(
        grad_update.dtype
    )
    grad_padded = with_halo(grad_wide.astype(jnp.bfloat16), (("lat", 1),), 3, False).astype(
        grad_wide.dtype
    )
    grad_fields = (
        grad_update + spread(grad_padded, conv_weight[::-1, ::-1], lat_rows, lon_cols)
    ).astype(jnp.bfloat16)
    grad_conv = correlate(padded, grad_update, lat_rows, lon_cols)
    totals = lax.psum((grad_weight, grad_out, grad_conv, grad_gain), ("lon", "lat", "dp"))
    return (result, grad_fields, totals[0], totals[1], totals[2], totals[3])


MESH = pl.DeviceIdType.MESH
AXES = ("lat", "lon", "dp")
LANES = 128


def place():
    return tuple(lax.axis_index(a) for a in AXES)


def greet(sizes):
    me = place()
    barrier = pltpu.get_barrier_semaphore()
    count = 0
    for offset in itertools.product(*(range(s) for s in sizes)):
        if not any(offset):
            continue
        target = {a: lax.rem(m + o, s) for a, m, o, s in zip(AXES, me, offset, sizes)}
        pl.semaphore_signal(barrier, inc=1, device_id=target, device_id_type=MESH)
        count += 1
    pl.semaphore_wait(barrier, count)


def remote(src, dst, send, recv, target):
    return pltpu.make_async_remote_copy(
        src_ref=src, dst_ref=dst, send_sem=send, recv_sem=recv, device_id=target, device_id_type=MESH
    )


def bring_rows(sizes, f_ref, c_ref, fp_ref, cr_ref, send, recv, xsend, xrecv):
    n_lat, n_lon, _ = sizes
    lat, lon, _ = place()
    rows = f_ref.shape[0]
    own = rows // n_lon

    def fields_copy(i, j):
        low, high = max(0, own * j - 3), min(rows, own * j + own + 3)
        start = low - (own * j - 3)
        return remote(
            f_ref.at[low:high],
            fp_ref.at[start : start + high - low, i],
            send.at[0, j],
            recv.at[0, i],
            {"lon": j},
        )

    def cot_copy(i, j):
        return remote(
            c_ref.at[own * j : own * j + own], cr_ref.at[:, i], send.at[1, j], recv.at[1, i], {"lon": j}
        )

    def below(i):
        return remote(
            f_ref.at[rows - 3 : rows], fp_ref.at[0:3, i], xsend.at[0], xrecv.at[0, i],
            {"lat": lat + 1, "lon": 0},
        )

    def above(i):
        return remote(
            f_ref.at[0:3], fp_ref.at[own + 3 : own + 6, i], xsend.at[1], xrecv.at[1, i],
            {"lat": lat - 1, "lon": n_lon - 1},
        )

    greet(sizes)

    @pl.when(lat < n_lat - 1)
    def _():
        below(lon).start()

    @pl.when(lat > 0)
    def _():
        above(lon).start()

    for j in range(n_lon):

        @pl.when(lon != j)
        def _(j=j):
            fields_copy(lon, j).start()

    for j in range(n_lon):

        @pl.when(lon != j)
        def _(j=j):
            cot_copy(lon, j).start()

        @pl.when(lon == j)
        def _(j=j):
            low, high = max(0, own * j - 3), min(rows, own * j + own + 3)
            start = low - (own * j - 3)
            fp_ref[start : start + high - low, j] = f_ref[low:high]
            cr_ref[:, j] = c_ref[own * j : own * j + own]

    @pl.when((lat == 0) & (lon == 0))
    def _():
        fp_ref[0:3] = jnp.zeros((3,) + fp_ref.shape[1:], fp_ref.dtype)

    @pl.when((lat == n_lat - 1) & (lon == n_lon - 1))
    def _():
        fp_ref[own + 3 : own + 6] = jnp.zeros((3,) + fp_ref.shape[1:], fp_ref.dtype)

    for j in range(n_lon):

        @pl.when(lon == j)
        def _(j=j):
            for i in range(n_lon):
                if i != j:
                    fields_copy(i, j).wait_recv()
                    cot_copy(i, j).wait_recv()

        @pl.when(lon != j)
        def _(j=j):
            fields_copy(lon, j).wait_send()
            cot_copy(lon, j).wait_send()

    @pl.when((lat > 0) & (lon == 0))
    def _():
        for i in range(n_lon):
            below(i).wait_recv()

    @pl.when((lat < n_lat - 1) & (lon == n_lon - 1))
    def _():
        for i in range(n_lon):
            above(i).wait_recv()

    @pl.when(lat < n_lat - 1)
    def _():
        below(lon).wait_send()

    @pl.when(lat > 0)
    def _():
        above(lon).wait_send()


def convolve(pad, weight, out, own, flip):
    circle, channels = pad.shape[1], pad.shape[2]
    for c in range(channels // LANES):
        lanes = slice(c * LANES, (c + 1) * LANES)

        def row(r, carry, lanes=lanes):
            bands = [pad[r + a, :, lanes] for a in range(7)]
            total = bands[3]
            for e in range(7):
                part = None
                for a in range(7):
                    tap = weight[(6 - a if flip else a) * 7 + e, :, lanes]
                    term = bands[a] * tap
                    part = term if part is None else part + term
                turn = (e - 3 if flip else 3 - e) % circle
                if turn:
                    part = pltpu.roll(part, turn, 0)
                total = total + part
            out[r, :, lanes] = total
            return carry

        lax.fori_loop(0, own, row, 0)


def correlate_rows(pad, upstream, out, own):
    circle, channels = pad.shape[1], pad.shape[2]

    def chunk(c, carry):
        lanes = pl.ds(pl.multiple_of(c * LANES, LANES), LANES)
        for e in range(7):
            turn = (e - 3) % circle
            turned = [upstream[r, :, lanes] for r in range(own)]
            if turn:
                turned = [pltpu.roll(t, turn, 0) for t in turned]
            for a in range(7):
                total = None
                for r in range(own):
                    term = pad[r + a, :, lanes] * turned[r]
                    total = term if total is None else total + term
                out[a * 7 + e, :, lanes] = jnp.sum(total, axis=0, keepdims=True)
        return carry

    lax.fori_loop(0, channels // LANES, chunk, 0)


def dot(left, right, dims):
    return lax.dot_general(left, right, (dims, ((), ())), preferred_element_type=jnp.float32)


PLAIN, COLS, ROWS = ((1,), (0,)), ((1,), (1,)), ((0,), (0,))


def attend_rows(projected, grad_mixed, circle, att_width):
    cells = projected.shape[0]
    group = max(circle, LANES)
    row_of = lax.broadcasted_iota(jnp.int32, (group, group), 0) // circle
    col_of = lax.broadcasted_iota(jnp.int32, (group, group), 1) // circle
    same = row_of == col_of
    lane_head = lax.broadcasted_iota(jnp.int32, (group, LANES), 1) // HEAD_DIM
    bf16 = jnp.bfloat16
    mixed, grads = [], []
    for g in range(cells // group):
        cut = slice(g * group, (g + 1) * group)
        mixed_row, grad_q, grad_k, grad_v = [], [], [], []
        for pair in range(att_width // LANES):
            at = slice(pair * LANES, (pair + 1) * LANES)
            q = projected[cut, :att_width][:, at]
            k = projected[cut, att_width : 2 * att_width][:, at]
            v = projected[cut, 2 * att_width :][:, at]
            up = grad_mixed[cut, at]
            parts = [[], [], [], []]
            for h in range(LANES // HEAD_DIM):
                mine = lane_head == h
                zero = jnp.zeros((), bf16)
                scores = dot(jnp.where(mine, q, zero), k, COLS) * HEAD_DIM ** (-0.5)
                scores = jnp.where(same, scores, -jnp.inf)
                raised = jnp.exp(scores - jnp.max(scores, -1, keepdims=True))
                probs = raised / jnp.sum(raised, -1, keepdims=True)
                weights = probs.astype(bf16)
                grad_probs = dot(jnp.where(mine, up, zero), v, COLS)
                inner = jnp.sum(probs * grad_probs, -1, keepdims=True)
                grad_scores = (probs * (grad_probs - inner) * HEAD_DIM ** (-0.5)).astype(bf16)
                parts[0].append(dot(weights, v, PLAIN))
                parts[1].append(dot(grad_scores, k, PLAIN))
                parts[2].append(dot(grad_scores, q, ROWS))
                parts[3].append(dot(weights, up, ROWS))
            for part, found in zip(parts, (mixed_row, grad_q, grad_k, grad_v)):
                whole = part[0]
                for h in range(1, len(part)):
                    whole = jnp.where(lane_head == h, part[h], whole)
                found.append(whole.astype(bf16))
        mixed.append(jnp.concatenate(mixed_row, axis=1))
        grads.append(jnp.concatenate(grad_q + grad_k + grad_v, axis=1))
    return jnp.concatenate(mixed, axis=0), jnp.concatenate(grads, axis=0)


def core_step(fp_ref, cr_ref, weight, gain_ref, wq_ref, wo_ref,
              result_ref, gu_ref, gub_ref, gq_ref, go_ref, gg_ref, pad, update_ref):
    own, blocks, width, channels = cr_ref.shape
    circle, cells = blocks * width, own * blocks * width
    att_width = wo_ref.shape[0]
    pad[...] = fp_ref[...].astype(jnp.float32).reshape(pad.shape)
    convolve(pad, weight, update_ref, own, False)
    update = update_ref[...].reshape(cells, channels)
    gain = gain_ref[...]
    inverse = lax.rsqrt(jnp.mean(update * update, -1, keepdims=True) + EPSILON)
    normed = (update * inverse * gain).astype(jnp.bfloat16)
    projected = dot(normed, wq_ref[...], PLAIN).astype(jnp.bfloat16)
    cot32 = cr_ref[...].astype(jnp.float32).reshape(cells, channels)
    cot = cot32.astype(jnp.bfloat16)
    grad_mixed = dot(cot, wo_ref[...], COLS).astype(jnp.bfloat16)
    mixed, grad_projected = attend_rows(projected, grad_mixed, circle, att_width)
    result = update + dot(mixed, wo_ref[...], PLAIN)
    result_ref[...] = result.reshape(result_ref.shape).astype(jnp.bfloat16)
    go_ref[...] = dot(mixed, cot, ROWS)
    gq_ref[...] = dot(normed, grad_projected, ROWS)
    grad_normed = dot(grad_projected, wq_ref[...], COLS)
    gg_ref[...] = jnp.sum(grad_normed * (update * inverse), axis=0, keepdims=True)
    gained = gain * grad_normed
    grad_update = (
        cot32
        + inverse * gained
        - update * (inverse * inverse * inverse) * jnp.mean(gained * update, -1, keepdims=True)
    )
    gu_ref[...] = grad_update.reshape(gu_ref.shape)
    gub_ref[...] = grad_update.reshape(gub_ref.shape).astype(jnp.bfloat16)


def halo_rows(sizes, g_ref, top_ref, low_ref, send, recv):
    n_lat, n_lon, _ = sizes
    lat, lon, _ = place()
    own = g_ref.shape[0]
    index, last = lat * n_lon + lon, n_lat * n_lon - 1

    def at(k):
        k = lax.rem(k + n_lat * n_lon, n_lat * n_lon)
        return {"lat": k // n_lon, "lon": lax.rem(k, n_lon)}

    down = remote(g_ref.at[own - 3 : own], top_ref, send.at[0], recv.at[0], at(index + 1))
    up = remote(g_ref.at[0:3], low_ref, send.at[1], recv.at[1], at(index - 1))
    greet(sizes)

    @pl.when(index < last)
    def _():
        down.start()

    @pl.when(index > 0)
    def _():
        up.start()

    @pl.when(index == 0)
    def _():
        top_ref[...] = jnp.zeros_like(top_ref)

    @pl.when(index == last)
    def _():
        low_ref[...] = jnp.zeros_like(low_ref)

    @pl.when(index > 0)
    def _():
        down.wait_recv()
        up.wait_send()

    @pl.when(index < last)
    def _():
        up.wait_recv()
        down.wait_send()


def final_step(fp_ref, gu_ref, top_ref, low_ref, weight, gg_ref, gq_ref, go_ref,
               gf_ref, big_ref, pad, gpad, out, conv):
    own, circle, channels = gu_ref.shape
    pad[...] = fp_ref[...].astype(jnp.float32).reshape(pad.shape)
    gpad[0:3] = top_ref[...].astype(jnp.float32).reshape((3, circle, channels))
    gpad[3 : own + 3] = gu_ref[...]
    gpad[own + 3 :] = low_ref[...].astype(jnp.float32).reshape((3, circle, channels))
    convolve(gpad, weight, out, own, True)
    gf_ref[...] = out[...].reshape(gf_ref.shape).astype(jnp.bfloat16)
    correlate_rows(pad, gu_ref, conv, own)
    pack(big_ref, gq_ref, go_ref, conv, gg_ref)


def pack(big_ref, gq_ref, go_ref, conv, gg_ref):
    parts, rows, _ = big_ref.shape
    whole = parts * rows
    wide = gq_ref.shape[1]
    att, channels = go_ref.shape
    bf16 = jnp.bfloat16
    fold = whole // att
    part = channels // fold
    big_ref[:, :, :wide] = gq_ref[...].reshape(parts, rows, wide).astype(bf16)
    small = jnp.concatenate([conv[k] for k in range(49)] + [gg_ref[...]], axis=0)
    small = jnp.concatenate([small, jnp.zeros((64 - 50, channels), jnp.float32)], axis=0)
    for k in range(fold):
        piece = go_ref[:, k * part : (k + 1) * part].astype(bf16).reshape(parts // fold, rows, part)
        big_ref[k * (parts // fold) : (k + 1) * (parts // fold), :, wide : wide + part] = piece
    step = 64 // rows
    big_ref[:, :, wide + part :] = jnp.zeros((parts, rows, LANES), bf16)
    for k in range(channels // LANES):
        piece = small[:, k * LANES : (k + 1) * LANES].astype(bf16).reshape(step, rows, LANES)
        big_ref[k * step : (k + 1) * step, :, wide + part :] = piece


def unpack(big, channels, wide, att):
    parts, rows, _ = big.shape
    whole = parts * rows
    flat = big.reshape(whole, -1).astype(jnp.float32)
    fold = whole // att
    part = channels // fold
    grad_weight = flat[:, :wide]
    grad_out = jnp.concatenate([flat[k * att : (k + 1) * att, wide : wide + part] for k in range(fold)], axis=1)
    small = jnp.concatenate(
        [flat[k * 64 : (k + 1) * 64, wide + part :] for k in range(channels // LANES)], axis=1
    )
    return grad_weight, grad_out, small[:49].reshape(7, 7, channels), small[49]


def give_rows(n_lon, lon, src, dst, send, recv):
    own = src.shape[0]

    def copy(i, j):
        return remote(src.at[:, j], dst.at[pl.ds(i * own, own)], send.at[j], recv.at[i], {"lon": j})

    def start():
        for j in range(n_lon):

            @pl.when(lon != j)
            def _(j=j):
                copy(lon, j).start()

            @pl.when(lon == j)
            def _(j=j):
                dst[j * own : (j + 1) * own] = src[:, j]

    def wait():
        for j in range(n_lon):

            @pl.when(lon == j)
            def _(j=j):
                for i in range(n_lon):
                    if i != j:
                        copy(i, j).wait_recv()

            @pl.when(lon != j)
            def _(j=j):
                copy(lon, j).wait_send()

    return start, wait


def sum_stages(sizes, big, all_ref, got1, sum1, got2, sum2, got3, send, recv):
    n_lat, n_lon, n_dp = sizes
    lat, lon, dp = place()
    half, quarter = n_lat * n_lon, n_lon
    f32 = jnp.float32
    other_dp, other_lat = 1 - dp, 1 - lat
    mine = dp * half + lat * quarter
    one = remote(big.at[pl.ds(other_dp * half, half)], got1, send.at[0], recv.at[0], {"dp": other_dp})
    two = remote(sum1.at[pl.ds(other_lat * quarter, quarter)], got2, send.at[1], recv.at[1], {"lat": other_lat})

    def three(i, j):
        return remote(sum2.at[j], got3.at[i], send.at[2 + j], recv.at[2 + i], {"lon": j})

    base = 2 + n_lon

    def four(i, j):
        spot = all_ref.at[mine + i]
        return remote(spot, spot, send.at[base + j], recv.at[base + i], {"lon": j})

    base2 = base + n_lon

    def five(side):
        spot = all_ref.at[pl.ds(dp * half + side * quarter, quarter)]
        return remote(spot, spot, send.at[base2], recv.at[base2], {"lat": other_lat})

    def six(side):
        spot = all_ref.at[pl.ds(side * half, half)]
        return remote(spot, spot, send.at[base2 + 1], recv.at[base2 + 1], {"dp": other_dp})

    def others(do):
        for j in range(n_lon):

            @pl.when(lon != j)
            def _(j=j):
                do(j)

    def s0():
        one.start()

    def s1():
        one.wait()
        for k in range(half):
            sum1[k] = (big[dp * half + k].astype(f32) + got1[k].astype(f32)).astype(sum1.dtype)
        two.start()

    def s2():
        two.wait()
        for k in range(quarter):
            sum2[k] = (sum1[lat * quarter + k].astype(f32) + got2[k].astype(f32)).astype(sum2.dtype)
        others(lambda j: three(lon, j).start())
        got3[lon] = sum2[lon]

    def s3():
        others(lambda j: three(j, j).wait_recv())
        others(lambda j: three(lon, j).wait_send())
        total = got3[0].astype(f32)
        for i in range(1, n_lon):
            total = total + got3[i].astype(f32)
        all_ref[mine + lon] = total.astype(all_ref.dtype)
        others(lambda j: four(lon, j).start())

    def s4():
        others(lambda j: four(j, j).wait_recv())
        others(lambda j: four(lon, j).wait_send())
        five(lat).start()

    def s5():
        five(lat).wait_send()
        five(other_lat).wait_recv()
        six(dp).start()

    def s6():
        six(dp).wait_send()
        six(other_dp).wait_recv()

    return s0, s1, s2, s3, s4, s5, s6


def send_back(sizes, result_ref, gf_ref, big, result_out, gf_out, all_ref,
              got1, sum1, got2, sum2, got3, send, recv, rsend, rrecv, gsend, grecv):
    lon = lax.axis_index("lon")
    stages = sum_stages(sizes, big, all_ref, got1, sum1, got2, sum2, got3, send, recv)
    start_r, wait_r = give_rows(sizes[1], lon, result_ref, result_out, rsend, rrecv)
    start_g, wait_g = give_rows(sizes[1], lon, gf_ref, gf_out, gsend, grecv)
    greet(sizes)
    stages[0]()
    start_g()
    start_r()
    for stage in stages[1:]:
        stage()
    wait_g()
    wait_r()


def call(body, outs, scratch, collective=None):
    def wrapped(*args):
        side = {} if collective is None else {"collective_id": collective, "has_side_effects": True}
        return pl.pallas_call(
            body,
            out_shape=outs,
            in_specs=[pl.BlockSpec(memory_space=pltpu.VMEM)] * len(args),
            out_specs=[pl.BlockSpec(memory_space=pltpu.VMEM)] * len(outs),
            scratch_shapes=scratch,
            compiler_params=pltpu.CompilerParams(vmem_limit_bytes=48 * 2**20, **side),
        )(*args)

    return wrapped


def on_device(sizes, fields, cotangent, conv_weight, norm_gain, w_qkv, w_out):
    n_lat, n_lon, n_dp = sizes
    batch, rows, cols, channels = fields.shape
    own, circle = rows // n_lon, cols * n_lon
    att = w_out.shape[0]
    bf16, f32 = jnp.bfloat16, jnp.float32
    shape = jax.ShapeDtypeStruct
    sems = pltpu.SemaphoreType.DMA
    taps = conv_weight.reshape(49, 1, channels)
    gain = norm_gain.reshape(1, channels)
    padded, cot = call(
        functools.partial(bring_rows, sizes),
        [shape((own + 6, n_lon, cols, channels), bf16), shape((own, n_lon, cols, channels), bf16)],
        [sems((2, n_lon)), sems((2, n_lon)), sems((2,)), sems((2, n_lon))],
        1,
    )(fields[0], cotangent[0])
    blocked = (own, n_lon, cols, channels)
    result, gu, gub, gq, go, gg = call(
        core_step,
        [shape(blocked, bf16), shape((own, circle, channels), f32), shape(blocked, bf16),
         shape(w_qkv.shape, f32), shape(w_out.shape, f32), shape((1, channels), f32)],
        [pltpu.VMEM((own + 6, circle, channels), f32), pltpu.VMEM((own, circle, channels), f32)],
    )(padded, cot, taps, gain, w_qkv, w_out)
    top, low = call(
        functools.partial(halo_rows, sizes),
        [shape((3,) + blocked[1:], bf16)] * 2,
        [sems((2,)), sems((2,))],
        2,
    )(gub)
    parts = n_lat * n_lon * n_dp
    part_rows = channels // parts
    wide = w_qkv.shape[1] + att * channels // channels + LANES
    pieces = lambda n: pltpu.VMEM((n, part_rows, wide), bf16)
    gf, big = call(
        final_step,
        [shape(blocked, bf16), shape((parts, part_rows, wide), bf16)],
        [pltpu.VMEM((own + 6, circle, channels), f32), pltpu.VMEM((own + 6, circle, channels), f32),
         pltpu.VMEM((own, circle, channels), f32), pltpu.VMEM((49, 1, channels), f32)],
    )(padded, gu, top, low, taps, gg, gq, go)
    result, grad_fields, total = call(
        functools.partial(send_back, sizes),
        [shape((rows, cols, channels), bf16)] * 2 + [shape((parts, part_rows, wide), bf16)],
        [pieces(parts // 2), pieces(parts // 2), pieces(n_lon), pieces(n_lon), pieces(n_lon),
         sems((4 + 2 * n_lon,)), sems((4 + 2 * n_lon,)),
         sems((n_lon,)), sems((n_lon,)), sems((n_lon,)), sems((n_lon,))],
        3,
    )(result, gf, big)
    grad_weight, grad_out, grad_conv, grad_gain = unpack(total, channels, w_qkv.shape[1], att)
    return result[None], grad_fields[None], grad_weight, grad_out, grad_conv, grad_gain


def pick(mesh, *args):
    sizes = tuple(mesh.shape[a] for a in AXES)
    _, rows, cols, channels = args[0].shape
    att = args[5].shape[0]
    n_lat, n_lon, n_dp = sizes
    parts = n_lat * n_lon * n_dp
    fits = (
        args[0].shape[0] == 1 and n_lat == 2 and n_dp == 2 and n_lon > 1
        and rows % n_lon == 0 and rows // n_lon >= 3 and cols % 8 == 0
        and LANES % (cols * n_lon) == 0 and (rows // n_lon * cols * n_lon) % LANES == 0
        and channels == 2 * att and channels % (8 * parts) == 0 and 64 % (channels // parts) == 0
        and att % LANES == 0
    )
    return on_device(sizes, *args) if fits else on_device_native(*args)


def solution(mesh):
    placed = (
        P(("member", "dp"), "lat", "lon", None),
        P(("member", "dp"), "lat", "lon", None),
        P(),
        P(),
        P(),
        P(),
    )
    return jax.shard_map(
        functools.partial(pick, mesh),
        mesh=mesh,
        in_specs=placed,
        out_specs=(
            P(("member", "dp"), "lat", "lon", None),
            P(("member", "dp"), "lat", "lon", None),
            P("member", None),
            P("member", None),
            P("member", None, None),
            P("member"),
        ),
        check_vma=False,
    )
```

```python
import functools
import itertools

import jax
import jax.numpy as jnp
from jax import lax
from jax.experimental import pallas as pl
from jax.experimental.pallas import tpu as pltpu
from jax.sharding import PartitionSpec as P

HEADS = 4
HEAD_DIM = 64


EPSILON = 1e-06


def with_halo(x, sides, width, wrap):
    for axis, dim in sides:
        size, length = (lax.axis_size(axis), x.shape[dim])
        up = [(i, (i + 1) % size) for i in range(size if wrap else size - 1)]
        down = [(j, i) for i, j in up]
        last = lax.slice_in_dim(x, length - width, length, axis=dim)
        first = lax.slice_in_dim(x, 0, width, axis=dim)
        before = lax.ppermute(last, axis, up)
        after = lax.ppermute(first, axis, down)
        x = jnp.concatenate([before, x, after], axis=dim)
    return x


def spread(padded, kernel, lat_rows, lon_cols):
    summed = jnp.zeros(padded.shape[:1] + (lat_rows, lon_cols, padded.shape[3]), jnp.float32)
    for row_shift in range(7):
        band = padded[:, row_shift : row_shift + lat_rows].astype(jnp.float32)
        partial_row = kernel[row_shift, 0] * band[:, :, 0:lon_cols]
        for col_shift in range(1, 7):
            partial_row = (
                partial_row
                + kernel[row_shift, col_shift] * band[:, :, col_shift : col_shift + lon_cols]
            )
        summed = summed + partial_row
    return summed


def correlate(padded, upstream, lat_rows, lon_cols):
    pieces = []
    for row_shift in range(7):
        for col_shift in range(7):
            window = padded[
                :, row_shift : row_shift + lat_rows, col_shift : col_shift + lon_cols
            ].astype(jnp.float32)
            pieces.append(jnp.sum(window * upstream, axis=(0, 1, 2)))
    return jnp.stack(pieces).reshape(7, 7, -1)


def split_heads(values):
    return values.reshape(values.shape[:-1] + (HEADS, HEAD_DIM))


def attend_forward(rowwise, att_width):
    queries = split_heads(rowwise[..., :att_width])
    keys_part = split_heads(rowwise[..., att_width : 2 * att_width])
    values_part = split_heads(rowwise[..., 2 * att_width :])
    scores = jnp.einsum(
        "brqhd,brkhd->brhqk", queries, keys_part, preferred_element_type=jnp.float32
    ) * HEAD_DIM ** (-0.5)
    row_peak = jnp.max(scores, -1, keepdims=True)
    raised = jnp.exp(scores - row_peak)
    probs = raised / jnp.sum(raised, -1, keepdims=True)
    weights = probs.astype(jnp.bfloat16)
    mixed = jnp.einsum(
        "brhqk,brkhd->brqhd", weights, values_part, preferred_element_type=jnp.float32
    )
    return (mixed.reshape(rowwise.shape[:3] + (att_width,)).astype(jnp.bfloat16), probs)


def attend_backward(rowwise, probs, grad_rowwise, att_width):
    queries = split_heads(rowwise[..., :att_width])
    keys_part = split_heads(rowwise[..., att_width : 2 * att_width])
    values_part = split_heads(rowwise[..., 2 * att_width :])
    grad_heads = split_heads(grad_rowwise)
    weights = probs.astype(jnp.bfloat16)
    grad_probs = jnp.einsum(
        "brqhd,brkhd->brhqk", grad_heads, values_part, preferred_element_type=jnp.float32
    )
    inner = jnp.sum(probs * grad_probs, -1, keepdims=True)
    grad_scores = (probs * (grad_probs - inner) * HEAD_DIM ** (-0.5)).astype(jnp.bfloat16)
    grad_query = jnp.einsum(
        "brhqk,brkhd->brqhd", grad_scores, keys_part, preferred_element_type=jnp.float32
    )
    grad_key = jnp.einsum(
        "brhqk,brqhd->brkhd", grad_scores, queries, preferred_element_type=jnp.float32
    )
    grad_value = jnp.einsum(
        "brhqk,brqhd->brkhd", weights, grad_heads, preferred_element_type=jnp.float32
    )
    shaped = rowwise.shape[:3] + (att_width,)
    return jnp.concatenate(
        [
            grad_query.reshape(shaped).astype(jnp.bfloat16),
            grad_key.reshape(shaped).astype(jnp.bfloat16),
            grad_value.reshape(shaped).astype(jnp.bfloat16),
        ],
        axis=-1,
    )


def contract_rows(left, right):
    return lax.dot_general(
        left, right, (((0,), (0,)), ((), ())), preferred_element_type=jnp.float32
    )


def contract_cols(left, right):
    return lax.dot_general(
        left, right, (((1,), (1,)), ((), ())), preferred_element_type=jnp.float32
    )


def on_device_native(fields, cotangent, conv_weight, norm_gain, w_qkv, w_out):
    batch_count, lat_rows, lon_cols, channels = fields.shape
    att_width = w_out.shape[0]
    wide = with_halo(fields, (("lon", 2),), 3, True)
    padded = with_halo(wide, (("lat", 1),), 3, False)
    update = fields.astype(jnp.float32) + spread(padded, conv_weight, lat_rows, lon_cols)
    inverse = lax.rsqrt(jnp.mean(update * update, -1, keepdims=True) + EPSILON)
    normed = (update * inverse * norm_gain).astype(jnp.bfloat16)
    normed_flat = normed.reshape(-1, channels)
    projected = jnp.dot(normed_flat, w_qkv, preferred_element_type=jnp.float32).astype(jnp.bfloat16)
    rowwise = lax.all_to_all(
        projected.reshape(batch_count, lat_rows, lon_cols, 3 * att_width),
        "lon",
        split_axis=1,
        concat_axis=2,
        tiled=True,
    )
    mixed_rows, probs = attend_forward(rowwise, att_width)
    mixed = lax.all_to_all(mixed_rows, "lon", split_axis=2, concat_axis=1, tiled=True)
    mixed_flat = mixed.reshape(-1, att_width)
    result = (
        update
        + jnp.dot(mixed_flat, w_out, preferred_element_type=jnp.float32).reshape(update.shape)
    ).astype(jnp.bfloat16)
    upstream_flat = cotangent.reshape(-1, channels)
    grad_mixed = contract_cols(upstream_flat, w_out).astype(jnp.bfloat16)
    grad_out = contract_rows(mixed_flat, upstream_flat)
    grad_rowwise = lax.all_to_all(
        grad_mixed.reshape(batch_count, lat_rows, lon_cols, att_width),
        "lon",
        split_axis=1,
        concat_axis=2,
        tiled=True,
    )
    grad_projected_rows = attend_backward(rowwise, probs, grad_rowwise, att_width)
    grad_projected = lax.all_to_all(
        grad_projected_rows, "lon", split_axis=2, concat_axis=1, tiled=True
    )
    grad_flat = grad_projected.reshape(-1, 3 * att_width)
    grad_weight = contract_rows(normed_flat, grad_flat)
    grad_normed = contract_cols(grad_flat, w_qkv).reshape(update.shape)
    grad_gain = jnp.sum(grad_normed * (update * inverse), axis=(0, 1, 2))
    gained = norm_gain * grad_normed
    grad_update = (
        cotangent.astype(jnp.float32)
        + inverse * gained
        - update * inverse**3 * jnp.mean(gained * update, -1, keepdims=True)
    )
    grad_wide = with_halo(grad_update.astype(jnp.bfloat16), (("lon", 2),), 3, True).astype(
        grad_update.dtype
    )
    grad_padded = with_halo(grad_wide.astype(jnp.bfloat16), (("lat", 1),), 3, False).astype(
        grad_wide.dtype
    )
    grad_fields = (
        grad_update + spread(grad_padded, conv_weight[::-1, ::-1], lat_rows, lon_cols)
    ).astype(jnp.bfloat16)
    grad_conv = correlate(padded, grad_update, lat_rows, lon_cols)
    totals = lax.psum((grad_weight, grad_out, grad_conv, grad_gain), ("lon", "lat", "dp"))
    return (result, grad_fields, totals[0], totals[1], totals[2], totals[3])


MESH = pl.DeviceIdType.MESH
AXES = ("lat", "lon", "dp")
LANES = 128


def place():
    return tuple(lax.axis_index(a) for a in AXES)


def greet(sizes):
    me = place()
    barrier = pltpu.get_barrier_semaphore()
    count = 0
    for offset in itertools.product(*(range(s) for s in sizes)):
        if not any(offset):
            continue
        target = {a: lax.rem(m + o, s) for a, m, o, s in zip(AXES, me, offset, sizes)}
        pl.semaphore_signal(barrier, inc=1, device_id=target, device_id_type=MESH)
        count += 1
    pl.semaphore_wait(barrier, count)


def remote(src, dst, send, recv, target):
    return pltpu.make_async_remote_copy(
        src_ref=src, dst_ref=dst, send_sem=send, recv_sem=recv, device_id=target, device_id_type=MESH
    )


def bring_rows(sizes, f_ref, c_ref, fp_ref, cr_ref, send, recv, xsend, xrecv, local):
    n_lat, n_lon, _ = sizes
    lat, lon, _ = place()
    rows = f_ref.shape[0]
    own = rows // n_lon

    def span(j):
        low, high = max(0, own * j - 3), min(rows, own * j + own + 3)
        start = low - (own * j - 3)
        return slice(low, high), slice(start, start + high - low)

    def fields_copy(i, j):
        there, here = span(j)
        return remote(f_ref.at[there], fp_ref.at[here, i], send.at[0, j], recv.at[0, i], {"lon": j})

    def cot_copy(i, j):
        return remote(
            c_ref.at[own * j : own * j + own], cr_ref.at[:, i], send.at[1, j], recv.at[1, i], {"lon": j}
        )

    def fields_own(j):
        there, here = span(j)
        return pltpu.make_async_copy(f_ref.at[there], fp_ref.at[here, j], local.at[0])

    def cot_own(j):
        return pltpu.make_async_copy(c_ref.at[own * j : own * j + own], cr_ref.at[:, j], local.at[1])

    def below(i):
        return remote(
            f_ref.at[rows - 3 : rows], fp_ref.at[0:3, i], xsend.at[0], xrecv.at[0, i],
            {"lat": lat + 1, "lon": 0},
        )

    def above(i):
        return remote(
            f_ref.at[0:3], fp_ref.at[own + 3 : own + 6, i], xsend.at[1], xrecv.at[1, i],
            {"lat": lat - 1, "lon": n_lon - 1},
        )

    def start():
        for j in range(n_lon):

            @pl.when(lon != j)
            def _(j=j):
                fields_copy(lon, j).start()

        @pl.when(lat < n_lat - 1)
        def _():
            below(lon).start()

        @pl.when(lat > 0)
        def _():
            above(lon).start()

        for j in range(n_lon):

            @pl.when(lon != j)
            def _(j=j):
                cot_copy(lon, j).start()

            @pl.when(lon == j)
            def _(j=j):
                fields_own(j).start()
                cot_own(j).start()

        @pl.when((lat == 0) & (lon == 0))
        def _():
            fp_ref[0:3] = jnp.zeros((3,) + fp_ref.shape[1:], fp_ref.dtype)

        @pl.when((lat == n_lat - 1) & (lon == n_lon - 1))
        def _():
            fp_ref[own + 3 : own + 6] = jnp.zeros((3,) + fp_ref.shape[1:], fp_ref.dtype)

    def wait_fields():
        for j in range(n_lon):

            @pl.when(lon == j)
            def _(j=j):
                fields_own(j).wait()
                for i in range(n_lon):
                    if i != j:
                        fields_copy(i, j).wait_recv()

        @pl.when((lat > 0) & (lon == 0))
        def _():
            for i in range(n_lon):
                below(i).wait_recv()

        @pl.when((lat < n_lat - 1) & (lon == n_lon - 1))
        def _():
            for i in range(n_lon):
                above(i).wait_recv()

    def wait_cot():
        for j in range(n_lon):

            @pl.when(lon == j)
            def _(j=j):
                cot_own(j).wait()
                for i in range(n_lon):
                    if i != j:
                        cot_copy(i, j).wait_recv()

    def wait_sent():
        for j in range(n_lon):

            @pl.when(lon != j)
            def _(j=j):
                fields_copy(lon, j).wait_send()
                cot_copy(lon, j).wait_send()

        @pl.when(lat < n_lat - 1)
        def _():
            below(lon).wait_send()

        @pl.when(lat > 0)
        def _():
            above(lon).wait_send()

    return start, wait_fields, wait_cot, wait_sent


def convolve(pad, weight, out, own, flip):
    circle, channels = pad.shape[1], pad.shape[2]
    for c in range(channels // LANES):
        lanes = slice(c * LANES, (c + 1) * LANES)

        def row(r, carry, lanes=lanes):
            bands = [pad[r + a, :, lanes] for a in range(7)]
            total = bands[3]
            for e in range(7):
                part = None
                for a in range(7):
                    tap = weight[6 - a if flip else a, (6 - e if flip else e) : (7 - e if flip else e + 1), lanes]
                    term = bands[a] * tap
                    part = term if part is None else part + term
                turn = (3 - e) % circle
                if turn:
                    part = pltpu.roll(part, turn, 0)
                total = total + part
            out[r, :, lanes] = total
            return carry

        lax.fori_loop(0, own, row, 0)


def correlate_rows(pad, upstream, out, own):
    circle, channels = pad.shape[1], pad.shape[2]

    def chunk(c, carry):
        lanes = pl.ds(pl.multiple_of(c * LANES, LANES), LANES)
        for e in range(7):
            turn = (e - 3) % circle
            turned = [upstream[r, :, lanes] for r in range(own)]
            if turn:
                turned = [pltpu.roll(t, turn, 0) for t in turned]
            for a in range(7):
                total = None
                for r in range(own):
                    term = pad[r + a, :, lanes] * turned[r]
                    total = term if total is None else total + term
                out[a, e : e + 1, lanes] = jnp.sum(total, axis=0, keepdims=True)
        return carry

    lax.fori_loop(0, channels // LANES, chunk, 0)


def dot(left, right, dims):
    return lax.dot_general(left, right, (dims, ((), ())), preferred_element_type=jnp.float32)


PLAIN, COLS, ROWS = ((1,), (0,)), ((1,), (1,)), ((0,), (0,))


def attend_rows(projected, grad_mixed, circle, att_width):
    cells = projected.shape[0]
    group = max(circle, LANES)
    row_of = lax.broadcasted_iota(jnp.int32, (group, group), 0) // circle
    col_of = lax.broadcasted_iota(jnp.int32, (group, group), 1) // circle
    same = row_of == col_of
    lane_head = lax.broadcasted_iota(jnp.int32, (group, LANES), 1) // HEAD_DIM
    bf16 = jnp.bfloat16
    mixed, grads = [], []
    for g in range(cells // group):
        cut = slice(g * group, (g + 1) * group)
        mixed_row, grad_q, grad_k, grad_v = [], [], [], []
        for pair in range(att_width // LANES):
            at = slice(pair * LANES, (pair + 1) * LANES)
            q = projected[cut, :att_width][:, at]
            k = projected[cut, att_width : 2 * att_width][:, at]
            v = projected[cut, 2 * att_width :][:, at]
            up = grad_mixed[cut, at]
            parts = [[], [], [], []]
            for h in range(LANES // HEAD_DIM):
                mine = lane_head == h
                zero = jnp.zeros((), bf16)
                scores = dot(jnp.where(mine, q, zero), k, COLS) * HEAD_DIM ** (-0.5)
                scores = jnp.where(same, scores, -jnp.inf)
                raised = jnp.exp(scores - jnp.max(scores, -1, keepdims=True))
                probs = raised / jnp.sum(raised, -1, keepdims=True)
                weights = probs.astype(bf16)
                grad_probs = dot(jnp.where(mine, up, zero), v, COLS)
                inner = jnp.sum(probs * grad_probs, -1, keepdims=True)
                grad_scores = (probs * (grad_probs - inner) * HEAD_DIM ** (-0.5)).astype(bf16)
                parts[0].append(dot(weights, v, PLAIN))
                parts[1].append(dot(grad_scores, k, PLAIN))
                parts[2].append(dot(grad_scores, q, ROWS))
                parts[3].append(dot(weights, up, ROWS))
            for part, found in zip(parts, (mixed_row, grad_q, grad_k, grad_v)):
                whole = part[0]
                for h in range(1, len(part)):
                    whole = jnp.where(lane_head == h, part[h], whole)
                found.append(whole.astype(bf16))
        mixed.append(jnp.concatenate(mixed_row, axis=1))
        grads.append(jnp.concatenate(grad_q + grad_k + grad_v, axis=1))
    return jnp.concatenate(mixed, axis=0), jnp.concatenate(grads, axis=0)


def core_step(cr_ref, update_ref, gain, wq_ref, wo_ref, result_ref, gu_ref, gub_ref, gq_ref, go_ref, gg_ref):
    own, blocks, width, channels = cr_ref.shape
    circle, cells = blocks * width, own * blocks * width
    att_width = wo_ref.shape[0]
    update = update_ref[...].reshape(cells, channels)
    inverse = lax.rsqrt(jnp.mean(update * update, -1, keepdims=True) + EPSILON)
    normed = (update * inverse * gain).astype(jnp.bfloat16)
    projected = dot(normed, wq_ref[...], PLAIN).astype(jnp.bfloat16)
    yield
    cot32 = cr_ref[...].astype(jnp.float32).reshape(cells, channels)
    cot = cot32.astype(jnp.bfloat16)
    grad_mixed = dot(cot, wo_ref[...], COLS).astype(jnp.bfloat16)
    mixed, grad_projected = attend_rows(projected, grad_mixed, circle, att_width)
    grad_normed = dot(grad_projected, wq_ref[...], COLS)
    gained = gain * grad_normed
    grad_update = (
        cot32
        + inverse * gained
        - update * (inverse * inverse * inverse) * jnp.mean(gained * update, -1, keepdims=True)
    )
    gu_ref[...] = grad_update.reshape(gu_ref.shape)
    gub_ref[...] = grad_update.reshape(gub_ref.shape).astype(jnp.bfloat16)
    yield
    result = update + dot(mixed, wo_ref[...], PLAIN)
    result_ref[...] = result.reshape(result_ref.shape).astype(jnp.bfloat16)
    yield
    gg_ref[...] = jnp.sum(grad_normed * (update * inverse), axis=0, keepdims=True)
    go_ref[...] = dot(mixed, cot, ROWS)
    gq_ref[...] = dot(normed, grad_projected, ROWS)
    yield


def halo_rows(sizes, g_ref, top_ref, low_ref, send, recv):
    n_lat, n_lon, _ = sizes
    lat, lon, _ = place()
    own = g_ref.shape[0]
    index, last = lat * n_lon + lon, n_lat * n_lon - 1

    def at(k):
        k = lax.rem(k + n_lat * n_lon, n_lat * n_lon)
        return {"lat": k // n_lon, "lon": lax.rem(k, n_lon)}

    down = remote(g_ref.at[own - 3 : own], top_ref, send.at[0], recv.at[0], at(index + 1))
    up = remote(g_ref.at[0:3], low_ref, send.at[1], recv.at[1], at(index - 1))

    def start():
        @pl.when(index < last)
        def _():
            down.start()

        @pl.when(index > 0)
        def _():
            up.start()

        @pl.when(index == 0)
        def _():
            top_ref[...] = jnp.zeros_like(top_ref)

        @pl.when(index == last)
        def _():
            low_ref[...] = jnp.zeros_like(low_ref)

    def wait():
        @pl.when(index > 0)
        def _():
            down.wait_recv()
            up.wait_send()

        @pl.when(index < last)
        def _():
            up.wait_recv()
            down.wait_send()

    return start, wait


def pack(bigs, gq_ref, go_ref, conv, gg_ref):
    parts, rows, first = bigs[0].shape
    whole = parts * rows
    wide = gq_ref.shape[1]
    att, channels = go_ref.shape
    bf16 = jnp.bfloat16
    fold = whole // att
    part = channels // fold
    rest = wide - first
    bigs[0][...] = gq_ref[:, :first].reshape(parts, rows, first).astype(bf16)
    bigs[1][:, :, :rest] = gq_ref[:, first:].reshape(parts, rows, rest).astype(bf16)
    for k in range(fold):
        piece = go_ref[:, k * part : (k + 1) * part].astype(bf16).reshape(parts // fold, rows, part)
        bigs[1][k * (parts // fold) : (k + 1) * (parts // fold), :, rest : rest + part] = piece
    small = jnp.concatenate(
        [conv[a] for a in range(7)] + [gg_ref[...], jnp.zeros((64 - 50, channels), jnp.float32)], axis=0
    )
    step = 64 // rows
    bigs[1][:, :, rest + part :] = jnp.zeros((parts, rows, LANES), bf16)
    for k in range(channels // LANES):
        piece = small[:, k * LANES : (k + 1) * LANES].astype(bf16).reshape(step, rows, LANES)
        bigs[1][k * step : (k + 1) * step, :, rest + part :] = piece


def finish(one_ref, two_ref, result_ref, gf_ref, result_out, gf_out, gq_out, go_out, gc_out, gg_out):
    parts, rows, first = one_ref.shape
    whole = parts * rows
    wide = gq_out.shape[1]
    att, channels = go_out.shape
    fold = whole // att
    part = channels // fold
    rest = wide - first
    f32 = jnp.float32
    result_out[...] = result_ref[...]
    gf_out[...] = gf_ref[...]
    gq_out[:, :first] = one_ref[...].astype(f32).reshape(whole, first)
    gq_out[:, first:] = two_ref[:, :, :rest].astype(f32).reshape(whole, rest)
    for k in range(fold):
        piece = two_ref[k * (parts // fold) : (k + 1) * (parts // fold), :, rest : rest + part]
        go_out[:, k * part : (k + 1) * part] = piece.astype(f32).reshape(att, part)
    step = 64 // rows
    for k in range(channels // LANES):
        lanes = slice(k * LANES, (k + 1) * LANES)
        small = two_ref[k * step : (k + 1) * step, :, rest + part :].astype(f32).reshape(64, LANES)
        for a in range(7):
            gc_out[a, :, lanes] = small[a * 7 : (a + 1) * 7]
        gg_out[:, lanes] = small[49:50]


def halving(turns, big, every, got, held, send, recv):
    f32 = jnp.float32
    count = len(turns)
    sizes = [big.shape[0] >> (k + 1) for k in range(count)]
    base = [0]
    for n in sizes[:-1]:
        base.append(base[-1] + n)
    starts = [jnp.int32(0)]
    for (_, bit), n in zip(turns, sizes):
        starts.append(starts[-1] + bit * n)

    def source(k, at, n):
        return big.at[pl.ds(at, n)] if k == 0 else held.at[pl.ds(base[k - 1] + at, n)]

    def down(k):
        target, bit = turns[k]
        n = sizes[k]
        return remote(
            source(k, (1 - bit) * n, n), got.at[base[k] : base[k] + n], send.at[k], recv.at[k], target
        )

    def back(k, mine):
        target, bit = turns[k]
        n = sizes[k]
        spot = every.at[pl.ds(starts[k] + (bit if mine else 1 - bit) * n, n)]
        return remote(spot, spot, send.at[count + k], recv.at[count + k], target)

    def add(k):
        bit, n = turns[k][1], sizes[k]
        down(k).wait()
        for i in range(n):
            at = bit * n + i
            mine = big[at] if k == 0 else held[base[k - 1] + at]
            total = (mine.astype(f32) + got[base[k] + i].astype(f32)).astype(big.dtype)
            if k == count - 1:
                every[starts[count] + i] = total
            else:
                held[base[k] + i] = total
        if k == count - 1:
            back(k, True).start()
        else:
            down(k + 1).start()

    def gather(k):
        back(k, True).wait_send()
        back(k, False).wait_recv()
        if k:
            back(k - 1, True).start()

    stages = [lambda: down(0).start()]
    stages += [functools.partial(add, k) for k in range(count)]
    stages += [functools.partial(gather, k) for k in reversed(range(count))]
    return stages


def give_rows(n_lon, lon, src, dst, send, recv):
    own = src.shape[0]

    def copy(i, j):
        return remote(src.at[:, j], dst.at[pl.ds(i * own, own)], send.at[j], recv.at[i], {"lon": j})

    def start():
        for j in range(n_lon):

            @pl.when(lon != j)
            def _(j=j):
                copy(lon, j).start()

            @pl.when(lon == j)
            def _(j=j):
                dst[j * own : (j + 1) * own] = src[:, j]

    def wait():
        for j in range(n_lon):

            @pl.when(lon == j)
            def _(j=j):
                for i in range(n_lon):
                    if i != j:
                        copy(i, j).wait_recv()

            @pl.when(lon != j)
            def _(j=j):
                copy(lon, j).wait_send()

    return start, wait


def layer(sizes, f_ref, c_ref, w_hbm, gain_ref, wq_hbm, wo_hbm,
          result_out, gf_out, every1, every2,
          fp, cr, weight, wq, wo, pad, update, result, gu, gub, gq, go, gg, top, low, gpad, out, gf, conv,
          big1, got1, held1, big2, got2, held2,
          send, recv, xsend, xrecv, local, hsend, hrecv, rsend, rrecv, gsend, grecv, s1, r1, s2, r2):
    n_lat, n_lon, _ = sizes
    lat, lon, dp = place()
    own, circle, channels = gu.shape
    f32, bf16 = jnp.float32, jnp.bfloat16
    loads = [
        pltpu.make_async_copy(src, dst, local.at[2 + k])
        for k, (src, dst) in enumerate(((w_hbm, weight), (wq_hbm, wq), (wo_hbm, wo)))
    ]
    for load in loads:
        load.start()
    odd, high = lax.rem(lon, 2), lon // 2
    by_dp = ({"dp": 1 - dp}, dp)
    by_lat = ({"lat": 1 - lat}, lat)
    by_odd = ({"lon": lon + 1 - 2 * odd}, odd)
    by_high = ({"lon": lon + 2 - 4 * high}, high)
    one = halving((by_dp, by_lat, by_odd, by_high), big1, every1, got1, held1, s1, r1)
    two = halving((by_dp, by_odd, by_high, by_lat), big2, every2, got2, held2, s2, r2)
    start_in, wait_fields, wait_cot, wait_sent = bring_rows(
        sizes, f_ref, c_ref, fp, cr, send, recv, xsend, xrecv, local
    )
    start_h, wait_h = halo_rows(sizes, gub, top, low, hsend, hrecv)
    start_r, wait_r = give_rows(n_lon, lon, result, result_out, rsend, rrecv)
    start_g, wait_g = give_rows(n_lon, lon, gf, gf_out, gsend, grecv)
    greet(sizes)
    start_in()
    loads[0].wait()
    wait_fields()
    pad[...] = fp[...].astype(f32).reshape(pad.shape)
    convolve(pad, weight, update, own, False)
    for load in loads[1:]:
        load.wait()
    steps = core_step(cr, update, gain_ref[...], wq, wo, result, gu, gub, gq, go, gg)
    next(steps)
    wait_cot()
    next(steps)
    start_h()
    next(steps)
    start_r()
    next(steps)
    correlate_rows(pad, gu, conv, own)
    pack((big1, big2), gq, go, conv, gg)
    one[0]()
    two[0]()
    wait_h()
    gpad[0:3] = top[...].astype(f32).reshape((3, circle, channels))
    gpad[3 : own + 3] = gu[...]
    gpad[own + 3 :] = low[...].astype(f32).reshape((3, circle, channels))
    one[1]()
    two[1]()
    convolve(gpad, weight, out, own, True)
    gf[...] = out[...].reshape(gf.shape).astype(bf16)
    start_g()
    for stage_one, stage_two in zip(one[2:], two[2:]):
        stage_one()
        stage_two()
    wait_sent()
    wait_r()
    wait_g()


def on_device(sizes, fields, cotangent, conv_weight, norm_gain, w_qkv, w_out):
    n_lat, n_lon, n_dp = sizes
    batch, rows, cols, channels = fields.shape
    own, circle = rows // n_lon, cols * n_lon
    att = w_out.shape[0]
    bf16, f32 = jnp.bfloat16, jnp.float32
    shape = jax.ShapeDtypeStruct
    sems = pltpu.SemaphoreType.DMA
    vmem = pltpu.VMEM
    parts = n_lat * n_lon * n_dp
    part_rows = channels // parts
    wide = w_qkv.shape[1] + att * att // channels * (channels // att) + LANES
    first = (wide // LANES + 1) // 2 * LANES
    widths = (first, wide - first)
    turns = 2 + 2
    blocked = (own, n_lon, cols, channels)
    flat = (own, circle, channels)
    padded = (own + 6, circle, channels)
    sums = []
    for w in widths:
        sums += [vmem((n, part_rows, w), bf16) for n in (parts, parts, parts)]
    inside = pl.BlockSpec(memory_space=pltpu.VMEM)
    outside = pl.BlockSpec(memory_space=pl.ANY)
    result, grad_fields, one, two = pl.pallas_call(
        functools.partial(layer, sizes),
        out_shape=[shape((rows, cols, channels), bf16)] * 2
        + [shape((parts, part_rows, w), bf16) for w in widths],
        in_specs=[outside, outside, outside, inside, outside, outside],
        out_specs=[inside] * 4,
        scratch_shapes=[
            vmem((own + 6,) + blocked[1:], bf16), vmem(blocked, bf16), vmem(conv_weight.shape, f32),
            vmem(w_qkv.shape, bf16), vmem(w_out.shape, bf16),
            vmem(padded, f32), vmem(flat, f32), vmem(blocked, bf16), vmem(flat, f32), vmem(blocked, bf16),
            vmem(w_qkv.shape, f32), vmem(w_out.shape, f32), vmem((1, channels), f32),
            vmem((3,) + blocked[1:], bf16), vmem((3,) + blocked[1:], bf16),
            vmem(padded, f32), vmem(flat, f32), vmem(blocked, bf16), vmem(conv_weight.shape, f32),
        ] + sums + [
            sems((2, n_lon)), sems((2, n_lon)), sems((2,)), sems((2, n_lon)), sems((5,)),
            sems((2,)), sems((2,)),
            sems((n_lon,)), sems((n_lon,)), sems((n_lon,)), sems((n_lon,)),
            sems((2 * turns,)), sems((2 * turns,)), sems((2 * turns,)), sems((2 * turns,)),
        ],
        compiler_params=pltpu.CompilerParams(
            vmem_limit_bytes=48 * 2**20, collective_id=1, has_side_effects=True
        ),
    )(fields[0], cotangent[0], conv_weight, norm_gain.reshape(1, channels), w_qkv, w_out)
    outs = pl.pallas_call(
        finish,
        out_shape=[shape((rows, cols, channels), bf16)] * 2
        + [shape(w_qkv.shape, f32), shape(w_out.shape, f32), shape(conv_weight.shape, f32),
           shape((1, channels), f32)],
        in_specs=[inside] * 4,
        out_specs=[inside] * 6,
        compiler_params=pltpu.CompilerParams(vmem_limit_bytes=32 * 2**20),
    )(one, two, result, grad_fields)
    return outs[0][None], outs[1][None], outs[2], outs[3], outs[4], outs[5].reshape(channels)


def pick(mesh, *args):
    sizes = tuple(mesh.shape[a] for a in AXES)
    _, rows, cols, channels = args[0].shape
    att = args[5].shape[0]
    n_lat, n_lon, n_dp = sizes
    parts = n_lat * n_lon * n_dp
    fits = (
        args[0].shape[0] == 1 and n_lat == 2 and n_dp == 2 and n_lon == 4
        and rows % n_lon == 0 and rows // n_lon >= 3 and cols % 8 == 0
        and LANES % (cols * n_lon) == 0 and (rows // n_lon * cols * n_lon) % LANES == 0
        and channels == 2 * att and channels % (8 * parts) == 0 and 64 % (channels // parts) == 0
        and att % LANES == 0
    )
    return on_device(sizes, *args) if fits else on_device_native(*args)


def solution(mesh):
    placed = (
        P(("member", "dp"), "lat", "lon", None),
        P(("member", "dp"), "lat", "lon", None),
        P(),
        P(),
        P(),
        P(),
    )
    return jax.shard_map(
        functools.partial(pick, mesh),
        mesh=mesh,
        in_specs=placed,
        out_specs=(
            P(("member", "dp"), "lat", "lon", None),
            P(("member", "dp"), "lat", "lon", None),
            P("member", None),
            P("member", None),
            P("member", None, None),
            P("member"),
        ),
        check_vma=False,
    )
```

```python
import functools
import itertools

import jax
import jax.numpy as jnp
from jax import lax
from jax.experimental import pallas as pl
from jax.experimental.pallas import tpu as pltpu
from jax.sharding import PartitionSpec as P

HEADS = 4
HEAD_DIM = 64


EPSILON = 1e-06


def with_halo(x, sides, width, wrap):
    for axis, dim in sides:
        size, length = (lax.axis_size(axis), x.shape[dim])
        up = [(i, (i + 1) % size) for i in range(size if wrap else size - 1)]
        down = [(j, i) for i, j in up]
        last = lax.slice_in_dim(x, length - width, length, axis=dim)
        first = lax.slice_in_dim(x, 0, width, axis=dim)
        before = lax.ppermute(last, axis, up)
        after = lax.ppermute(first, axis, down)
        x = jnp.concatenate([before, x, after], axis=dim)
    return x


def spread(padded, kernel, lat_rows, lon_cols):
    summed = jnp.zeros(padded.shape[:1] + (lat_rows, lon_cols, padded.shape[3]), jnp.float32)
    for row_shift in range(7):
        band = padded[:, row_shift : row_shift + lat_rows].astype(jnp.float32)
        partial_row = kernel[row_shift, 0] * band[:, :, 0:lon_cols]
        for col_shift in range(1, 7):
            partial_row = (
                partial_row
                + kernel[row_shift, col_shift] * band[:, :, col_shift : col_shift + lon_cols]
            )
        summed = summed + partial_row
    return summed


def correlate(padded, upstream, lat_rows, lon_cols):
    pieces = []
    for row_shift in range(7):
        for col_shift in range(7):
            window = padded[
                :, row_shift : row_shift + lat_rows, col_shift : col_shift + lon_cols
            ].astype(jnp.float32)
            pieces.append(jnp.sum(window * upstream, axis=(0, 1, 2)))
    return jnp.stack(pieces).reshape(7, 7, -1)


def split_heads(values):
    return values.reshape(values.shape[:-1] + (HEADS, HEAD_DIM))


def attend_forward(rowwise, att_width):
    queries = split_heads(rowwise[..., :att_width])
    keys_part = split_heads(rowwise[..., att_width : 2 * att_width])
    values_part = split_heads(rowwise[..., 2 * att_width :])
    scores = jnp.einsum(
        "brqhd,brkhd->brhqk", queries, keys_part, preferred_element_type=jnp.float32
    ) * HEAD_DIM ** (-0.5)
    row_peak = jnp.max(scores, -1, keepdims=True)
    raised = jnp.exp(scores - row_peak)
    probs = raised / jnp.sum(raised, -1, keepdims=True)
    weights = probs.astype(jnp.bfloat16)
    mixed = jnp.einsum(
        "brhqk,brkhd->brqhd", weights, values_part, preferred_element_type=jnp.float32
    )
    return (mixed.reshape(rowwise.shape[:3] + (att_width,)).astype(jnp.bfloat16), probs)


def attend_backward(rowwise, probs, grad_rowwise, att_width):
    queries = split_heads(rowwise[..., :att_width])
    keys_part = split_heads(rowwise[..., att_width : 2 * att_width])
    values_part = split_heads(rowwise[..., 2 * att_width :])
    grad_heads = split_heads(grad_rowwise)
    weights = probs.astype(jnp.bfloat16)
    grad_probs = jnp.einsum(
        "brqhd,brkhd->brhqk", grad_heads, values_part, preferred_element_type=jnp.float32
    )
    inner = jnp.sum(probs * grad_probs, -1, keepdims=True)
    grad_scores = (probs * (grad_probs - inner) * HEAD_DIM ** (-0.5)).astype(jnp.bfloat16)
    grad_query = jnp.einsum(
        "brhqk,brkhd->brqhd", grad_scores, keys_part, preferred_element_type=jnp.float32
    )
    grad_key = jnp.einsum(
        "brhqk,brqhd->brkhd", grad_scores, queries, preferred_element_type=jnp.float32
    )
    grad_value = jnp.einsum(
        "brhqk,brqhd->brkhd", weights, grad_heads, preferred_element_type=jnp.float32
    )
    shaped = rowwise.shape[:3] + (att_width,)
    return jnp.concatenate(
        [
            grad_query.reshape(shaped).astype(jnp.bfloat16),
            grad_key.reshape(shaped).astype(jnp.bfloat16),
            grad_value.reshape(shaped).astype(jnp.bfloat16),
        ],
        axis=-1,
    )


def contract_rows(left, right):
    return lax.dot_general(
        left, right, (((0,), (0,)), ((), ())), preferred_element_type=jnp.float32
    )


def contract_cols(left, right):
    return lax.dot_general(
        left, right, (((1,), (1,)), ((), ())), preferred_element_type=jnp.float32
    )


def on_device_native(fields, cotangent, conv_weight, norm_gain, w_qkv, w_out):
    batch_count, lat_rows, lon_cols, channels = fields.shape
    att_width = w_out.shape[0]
    wide = with_halo(fields, (("lon", 2),), 3, True)
    padded = with_halo(wide, (("lat", 1),), 3, False)
    update = fields.astype(jnp.float32) + spread(padded, conv_weight, lat_rows, lon_cols)
    inverse = lax.rsqrt(jnp.mean(update * update, -1, keepdims=True) + EPSILON)
    normed = (update * inverse * norm_gain).astype(jnp.bfloat16)
    normed_flat = normed.reshape(-1, channels)
    projected = jnp.dot(normed_flat, w_qkv, preferred_element_type=jnp.float32).astype(jnp.bfloat16)
    rowwise = lax.all_to_all(
        projected.reshape(batch_count, lat_rows, lon_cols, 3 * att_width),
        "lon",
        split_axis=1,
        concat_axis=2,
        tiled=True,
    )
    mixed_rows, probs = attend_forward(rowwise, att_width)
    mixed = lax.all_to_all(mixed_rows, "lon", split_axis=2, concat_axis=1, tiled=True)
    mixed_flat = mixed.reshape(-1, att_width)
    result = (
        update
        + jnp.dot(mixed_flat, w_out, preferred_element_type=jnp.float32).reshape(update.shape)
    ).astype(jnp.bfloat16)
    upstream_flat = cotangent.reshape(-1, channels)
    grad_mixed = contract_cols(upstream_flat, w_out).astype(jnp.bfloat16)
    grad_out = contract_rows(mixed_flat, upstream_flat)
    grad_rowwise = lax.all_to_all(
        grad_mixed.reshape(batch_count, lat_rows, lon_cols, att_width),
        "lon",
        split_axis=1,
        concat_axis=2,
        tiled=True,
    )
    grad_projected_rows = attend_backward(rowwise, probs, grad_rowwise, att_width)
    grad_projected = lax.all_to_all(
        grad_projected_rows, "lon", split_axis=2, concat_axis=1, tiled=True
    )
    grad_flat = grad_projected.reshape(-1, 3 * att_width)
    grad_weight = contract_rows(normed_flat, grad_flat)
    grad_normed = contract_cols(grad_flat, w_qkv).reshape(update.shape)
    grad_gain = jnp.sum(grad_normed * (update * inverse), axis=(0, 1, 2))
    gained = norm_gain * grad_normed
    grad_update = (
        cotangent.astype(jnp.float32)
        + inverse * gained
        - update * inverse**3 * jnp.mean(gained * update, -1, keepdims=True)
    )
    grad_wide = with_halo(grad_update.astype(jnp.bfloat16), (("lon", 2),), 3, True).astype(
        grad_update.dtype
    )
    grad_padded = with_halo(grad_wide.astype(jnp.bfloat16), (("lat", 1),), 3, False).astype(
        grad_wide.dtype
    )
    grad_fields = (
        grad_update + spread(grad_padded, conv_weight[::-1, ::-1], lat_rows, lon_cols)
    ).astype(jnp.bfloat16)
    grad_conv = correlate(padded, grad_update, lat_rows, lon_cols)
    totals = lax.psum((grad_weight, grad_out, grad_conv, grad_gain), ("lon", "lat", "dp"))
    return (result, grad_fields, totals[0], totals[1], totals[2], totals[3])


MESH = pl.DeviceIdType.MESH
AXES = ("lat", "lon", "dp")
LANES = 128


def place():
    return tuple(lax.axis_index(a) for a in AXES)


def greet(sizes):
    me = place()
    barrier = pltpu.get_barrier_semaphore()
    count = 0
    for offset in itertools.product(*(range(s) for s in sizes)):
        if not any(offset):
            continue
        target = {a: lax.rem(m + o, s) for a, m, o, s in zip(AXES, me, offset, sizes)}
        pl.semaphore_signal(barrier, inc=1, device_id=target, device_id_type=MESH)
        count += 1
    pl.semaphore_wait(barrier, count)


def remote(src, dst, send, recv, target):
    return pltpu.make_async_remote_copy(
        src_ref=src, dst_ref=dst, send_sem=send, recv_sem=recv, device_id=target, device_id_type=MESH
    )


def bring_rows(sizes, f_ref, c_ref, fp_ref, cr_ref, send, recv, xsend, xrecv, local):
    n_lat, n_lon, _ = sizes
    lat, lon, _ = place()
    rows = f_ref.shape[0]
    own = rows // n_lon

    def span(j):
        low, high = max(0, own * j - 3), min(rows, own * j + own + 3)
        start = low - (own * j - 3)
        return slice(low, high), slice(start, start + high - low)

    def fields_copy(i, j):
        there, here = span(j)
        return remote(f_ref.at[there], fp_ref.at[here, i], send.at[0, j], recv.at[0, i], {"lon": j})

    def cot_copy(i, j):
        return remote(
            c_ref.at[own * j : own * j + own], cr_ref.at[:, i], send.at[1, j], recv.at[1, i], {"lon": j}
        )

    def fields_own(j):
        there, here = span(j)
        return pltpu.make_async_copy(f_ref.at[there], fp_ref.at[here, j], local.at[0])

    def cot_own(j):
        return pltpu.make_async_copy(c_ref.at[own * j : own * j + own], cr_ref.at[:, j], local.at[1])

    def below(i):
        return remote(
            f_ref.at[rows - 3 : rows], fp_ref.at[0:3, i], xsend.at[0], xrecv.at[0, i],
            {"lat": lat + 1, "lon": 0},
        )

    def above(i):
        return remote(
            f_ref.at[0:3], fp_ref.at[own + 3 : own + 6, i], xsend.at[1], xrecv.at[1, i],
            {"lat": lat - 1, "lon": n_lon - 1},
        )

    def start():
        for j in range(n_lon):

            @pl.when(lon != j)
            def _(j=j):
                fields_copy(lon, j).start()

        @pl.when(lat < n_lat - 1)
        def _():
            below(lon).start()

        @pl.when(lat > 0)
        def _():
            above(lon).start()

        for j in range(n_lon):

            @pl.when(lon != j)
            def _(j=j):
                cot_copy(lon, j).start()

            @pl.when(lon == j)
            def _(j=j):
                fields_own(j).start()
                cot_own(j).start()

        @pl.when((lat == 0) & (lon == 0))
        def _():
            fp_ref[0:3] = jnp.zeros((3,) + fp_ref.shape[1:], fp_ref.dtype)

        @pl.when((lat == n_lat - 1) & (lon == n_lon - 1))
        def _():
            fp_ref[own + 3 : own + 6] = jnp.zeros((3,) + fp_ref.shape[1:], fp_ref.dtype)

    def wait_fields():
        for j in range(n_lon):

            @pl.when(lon == j)
            def _(j=j):
                fields_own(j).wait()
                for i in range(n_lon):
                    if i != j:
                        fields_copy(i, j).wait_recv()

        @pl.when((lat > 0) & (lon == 0))
        def _():
            for i in range(n_lon):
                below(i).wait_recv()

        @pl.when((lat < n_lat - 1) & (lon == n_lon - 1))
        def _():
            for i in range(n_lon):
                above(i).wait_recv()

    def wait_cot():
        for j in range(n_lon):

            @pl.when(lon == j)
            def _(j=j):
                cot_own(j).wait()
                for i in range(n_lon):
                    if i != j:
                        cot_copy(i, j).wait_recv()

    def wait_sent():
        for j in range(n_lon):

            @pl.when(lon != j)
            def _(j=j):
                fields_copy(lon, j).wait_send()
                cot_copy(lon, j).wait_send()

        @pl.when(lat < n_lat - 1)
        def _():
            below(lon).wait_send()

        @pl.when(lat > 0)
        def _():
            above(lon).wait_send()

    return start, wait_fields, wait_cot, wait_sent


def convolve(pad, weight, out, own, flip):
    circle, channels = pad.shape[1], pad.shape[2]
    for c in range(channels // LANES):
        lanes = slice(c * LANES, (c + 1) * LANES)

        def row(r, carry, lanes=lanes):
            bands = [pad[r + a, :, lanes] for a in range(7)]
            total = bands[3]
            for e in range(7):
                part = None
                for a in range(7):
                    tap = weight[6 - a if flip else a, (6 - e if flip else e) : (7 - e if flip else e + 1), lanes]
                    term = bands[a] * tap
                    part = term if part is None else part + term
                turn = (3 - e) % circle
                if turn:
                    part = pltpu.roll(part, turn, 0)
                total = total + part
            out[r, :, lanes] = total
            return carry

        lax.fori_loop(0, own, row, 0)


def correlate_rows(pad, upstream, out, own):
    circle, channels = pad.shape[1], pad.shape[2]

    def chunk(c, carry):
        lanes = pl.ds(pl.multiple_of(c * LANES, LANES), LANES)
        for e in range(7):
            turn = (e - 3) % circle
            turned = [upstream[r, :, lanes] for r in range(own)]
            if turn:
                turned = [pltpu.roll(t, turn, 0) for t in turned]
            for a in range(7):
                total = None
                for r in range(own):
                    term = pad[r + a, :, lanes] * turned[r]
                    total = term if total is None else total + term
                out[a, e : e + 1, lanes] = jnp.sum(total, axis=0, keepdims=True)
        return carry

    lax.fori_loop(0, channels // LANES, chunk, 0)


def dot(left, right, dims):
    return lax.dot_general(left, right, (dims, ((), ())), preferred_element_type=jnp.float32)


PLAIN, COLS, ROWS = ((1,), (0,)), ((1,), (1,)), ((0,), (0,))


def attend_rows(projected, circle, att_width):
    cells = projected.shape[0]
    group = max(circle, LANES)
    row_of = lax.broadcasted_iota(jnp.int32, (group, group), 0) // circle
    col_of = lax.broadcasted_iota(jnp.int32, (group, group), 1) // circle
    same = row_of == col_of
    lane_head = lax.broadcasted_iota(jnp.int32, (group, LANES), 1) // HEAD_DIM
    bf16 = jnp.bfloat16
    zero = jnp.zeros((), bf16)
    heads = range(LANES // HEAD_DIM)
    groups = [slice(g * group, (g + 1) * group) for g in range(cells // group)]
    pairs = [slice(p * LANES, (p + 1) * LANES) for p in range(att_width // LANES)]

    def third(k, cut, at):
        return projected[cut, k * att_width : (k + 1) * att_width][:, at]

    def join(parts):
        whole = parts[0]
        for h in heads[1:]:
            whole = jnp.where(lane_head == h, parts[h], whole)
        return whole.astype(bf16)

    kept, mixed = {}, []
    for g, cut in enumerate(groups):
        found = []
        for p, at in enumerate(pairs):
            q, k, v = (third(n, cut, at) for n in range(3))
            parts = []
            for h in heads:
                scores = dot(jnp.where(lane_head == h, q, zero), k, COLS) * HEAD_DIM ** (-0.5)
                scores = jnp.where(same, scores, -jnp.inf)
                raised = jnp.exp(scores - jnp.max(scores, -1, keepdims=True))
                probs = raised / jnp.sum(raised, -1, keepdims=True)
                kept[g, p, h] = probs
                parts.append(dot(probs.astype(bf16), v, PLAIN))
            found.append(join(parts))
        mixed.append(jnp.concatenate(found, axis=1))

    def backward(grad_mixed):
        grads = []
        for g, cut in enumerate(groups):
            found = [[], [], []]
            for p, at in enumerate(pairs):
                q, k, v = (third(n, cut, at) for n in range(3))
                up = grad_mixed[cut, at]
                parts = [[], [], []]
                for h in heads:
                    probs = kept[g, p, h]
                    grad_probs = dot(jnp.where(lane_head == h, up, zero), v, COLS)
                    inner = jnp.sum(probs * grad_probs, -1, keepdims=True)
                    grad_scores = (probs * (grad_probs - inner) * HEAD_DIM ** (-0.5)).astype(bf16)
                    parts[0].append(dot(grad_scores, k, PLAIN))
                    parts[1].append(dot(grad_scores, q, ROWS))
                    parts[2].append(dot(probs.astype(bf16), up, ROWS))
                for part, into in zip(parts, found):
                    into.append(join(part))
            grads.append(jnp.concatenate(found[0] + found[1] + found[2], axis=1))
        return jnp.concatenate(grads, axis=0)

    return jnp.concatenate(mixed, axis=0), backward


def core_step(cr_ref, update_ref, gain, wq_ref, wo_ref, result_ref, gu_ref, gub_ref, big1_ref, big3_ref, go_ref, gg_ref):
    own, blocks, width, channels = cr_ref.shape
    circle, cells = blocks * width, own * blocks * width
    att_width = wo_ref.shape[0]
    update = update_ref[...].reshape(cells, channels)
    inverse = lax.rsqrt(jnp.mean(update * update, -1, keepdims=True) + EPSILON)
    normed = (update * inverse * gain).astype(jnp.bfloat16)
    projected = dot(normed, wq_ref[...], PLAIN).astype(jnp.bfloat16)
    mixed, backward = attend_rows(projected, circle, att_width)
    result = update + dot(mixed, wo_ref[...], PLAIN)
    result_ref[...] = result.reshape(result_ref.shape).astype(jnp.bfloat16)
    yield
    cot32 = cr_ref[...].astype(jnp.float32).reshape(cells, channels)
    cot = cot32.astype(jnp.bfloat16)
    grad_mixed = dot(cot, wo_ref[...], COLS).astype(jnp.bfloat16)
    grad_projected = backward(grad_mixed)
    grad_normed = dot(grad_projected, wq_ref[...], COLS)
    gained = gain * grad_normed
    grad_update = (
        cot32
        + inverse * gained
        - update * (inverse * inverse * inverse) * jnp.mean(gained * update, -1, keepdims=True)
    )
    gu_ref[...] = grad_update.reshape(gu_ref.shape)
    gub_ref[...] = grad_update.reshape(gub_ref.shape).astype(jnp.bfloat16)
    yield
    grad_weight = dot(normed, grad_projected, ROWS).astype(jnp.bfloat16)
    half = big1_ref.shape[2]
    big1_ref[...] = grad_weight[:, :half].reshape(big1_ref.shape)
    big3_ref[...] = grad_weight[:, half:].reshape(big3_ref.shape)
    yield
    gg_ref[...] = jnp.sum(grad_normed * (update * inverse), axis=0, keepdims=True)
    go_ref[...] = dot(mixed, cot, ROWS)
    yield


def halo_rows(sizes, g_ref, top_ref, low_ref, send, recv):
    n_lat, n_lon, _ = sizes
    lat, lon, _ = place()
    own = g_ref.shape[0]
    index, last = lat * n_lon + lon, n_lat * n_lon - 1

    def at(k):
        k = lax.rem(k + n_lat * n_lon, n_lat * n_lon)
        return {"lat": k // n_lon, "lon": lax.rem(k, n_lon)}

    down = remote(g_ref.at[own - 3 : own], top_ref, send.at[0], recv.at[0], at(index + 1))
    up = remote(g_ref.at[0:3], low_ref, send.at[1], recv.at[1], at(index - 1))

    def start():
        @pl.when(index < last)
        def _():
            down.start()

        @pl.when(index > 0)
        def _():
            up.start()

        @pl.when(index == 0)
        def _():
            top_ref[...] = jnp.zeros_like(top_ref)

        @pl.when(index == last)
        def _():
            low_ref[...] = jnp.zeros_like(low_ref)

    def wait():
        @pl.when(index > 0)
        def _():
            down.wait_recv()
            up.wait_send()

        @pl.when(index < last)
        def _():
            up.wait_recv()
            down.wait_send()

    return start, wait


def pack(big, go_ref, conv, gg_ref):
    parts, rows, _ = big.shape
    att, channels = go_ref.shape
    bf16 = jnp.bfloat16
    fold = parts * rows // att
    part = channels // fold
    for k in range(fold):
        piece = go_ref[:, k * part : (k + 1) * part].astype(bf16).reshape(parts // fold, rows, part)
        big[k * (parts // fold) : (k + 1) * (parts // fold), :, :part] = piece
    small = jnp.concatenate(
        [conv[a] for a in range(7)] + [gg_ref[...], jnp.zeros((64 - 50, channels), jnp.float32)], axis=0
    )
    step = 64 // rows
    used = channels // LANES * step
    for k in range(channels // LANES):
        piece = small[:, k * LANES : (k + 1) * LANES].astype(bf16).reshape(step, rows, LANES)
        big[k * step : (k + 1) * step, :, part:] = piece
    if used < parts:
        big[used:, :, part:] = jnp.zeros((parts - used, rows, LANES), bf16)


def finish(one_ref, three_ref, two_ref, result_ref, gf_ref, result_out, gf_out, gq_out, go_out, gc_out, gg_out):
    parts, rows, _ = two_ref.shape
    att, channels = go_out.shape
    fold = parts * rows // att
    part = channels // fold
    f32 = jnp.float32
    result_out[...] = result_ref[...]
    gf_out[...] = gf_ref[...]
    half = one_ref.shape[2]
    gq_out[:, :half] = one_ref[...].astype(f32).reshape(parts * rows, half)
    gq_out[:, half:] = three_ref[...].astype(f32).reshape(parts * rows, half)
    for k in range(fold):
        piece = two_ref[k * (parts // fold) : (k + 1) * (parts // fold), :, :part]
        go_out[:, k * part : (k + 1) * part] = piece.astype(f32).reshape(att, part)
    step = 64 // rows
    for k in range(channels // LANES):
        lanes = slice(k * LANES, (k + 1) * LANES)
        small = two_ref[k * step : (k + 1) * step, :, part:].astype(f32).reshape(64, LANES)
        for a in range(7):
            gc_out[a, :, lanes] = small[a * 7 : (a + 1) * 7]
        gg_out[:, lanes] = small[49:50]


def give_rows(n_lon, lon, src, dst, send, recv):
    own = src.shape[0]

    def copy(i, j):
        return remote(src.at[:, j], dst.at[pl.ds(i * own, own)], send.at[j], recv.at[i], {"lon": j})

    def start():
        for j in range(n_lon):

            @pl.when(lon != j)
            def _(j=j):
                copy(lon, j).start()

            @pl.when(lon == j)
            def _(j=j):
                dst[j * own : (j + 1) * own] = src[:, j]

    def wait():
        for j in range(n_lon):

            @pl.when(lon == j)
            def _(j=j):
                for i in range(n_lon):
                    if i != j:
                        copy(i, j).wait_recv()

            @pl.when(lon != j)
            def _(j=j):
                copy(lon, j).wait_send()

    return start, wait


def sum_stages(sizes, big, all_ref, got1, sum1, got2, sum2, got3, send, recv):
    n_lat, n_lon, n_dp = sizes
    lat, lon, dp = place()
    half, quarter = n_lat * n_lon, n_lon
    f32 = jnp.float32
    other_dp, other_lat = 1 - dp, 1 - lat
    mine = dp * half + lat * quarter
    one = remote(big.at[pl.ds(other_dp * half, half)], got1, send.at[0], recv.at[0], {"dp": other_dp})
    two = remote(sum1.at[pl.ds(other_lat * quarter, quarter)], got2, send.at[1], recv.at[1], {"lat": other_lat})

    def three(i, j):
        return remote(sum2.at[j], got3.at[i], send.at[2 + j], recv.at[2 + i], {"lon": j})

    base = 2 + n_lon

    def four(i, j):
        spot = all_ref.at[mine + i]
        return remote(spot, spot, send.at[base + j], recv.at[base + i], {"lon": j})

    base2 = base + n_lon

    def five(side):
        spot = all_ref.at[pl.ds(dp * half + side * quarter, quarter)]
        return remote(spot, spot, send.at[base2], recv.at[base2], {"lat": other_lat})

    def six(side):
        spot = all_ref.at[pl.ds(side * half, half)]
        return remote(spot, spot, send.at[base2 + 1], recv.at[base2 + 1], {"dp": other_dp})

    def others(do):
        for j in range(n_lon):

            @pl.when(lon != j)
            def _(j=j):
                do(j)

    def s0():
        one.start()

    def s1():
        one.wait()
        for k in range(half):
            sum1[k] = (big[dp * half + k].astype(f32) + got1[k].astype(f32)).astype(sum1.dtype)
        two.start()

    def s2():
        two.wait()
        for k in range(quarter):
            sum2[k] = (sum1[lat * quarter + k].astype(f32) + got2[k].astype(f32)).astype(sum2.dtype)
        others(lambda j: three(lon, j).start())
        got3[lon] = sum2[lon]

    def s3():
        others(lambda j: three(j, j).wait_recv())
        others(lambda j: three(lon, j).wait_send())
        total = got3[0].astype(f32)
        for i in range(1, n_lon):
            total = total + got3[i].astype(f32)
        all_ref[mine + lon] = total.astype(all_ref.dtype)
        others(lambda j: four(lon, j).start())

    def s4():
        others(lambda j: four(j, j).wait_recv())
        others(lambda j: four(lon, j).wait_send())
        five(lat).start()

    def s5():
        five(lat).wait_send()
        five(other_lat).wait_recv()
        six(dp).start()

    def s6():
        six(dp).wait_send()
        six(other_dp).wait_recv()

    return s0, s1, s2, s3, s4, s5, s6


def layer(sizes, f_ref, c_ref, w_hbm, gain_ref, wq_hbm, wo_hbm,
          result_out, gf_out, every1, every3, every2,
          fp, cr, weight, wq, wo, pad, update, result, gu, gub, go, gg, top, low, gpad, out, gf, conv,
          big1, a1, b1, c1, d1, e1, big3, a3, b3, c3, d3, e3, big2, a2, b2, c2, d2, e2,
          send, recv, xsend, xrecv, local, hsend, hrecv, rsend, rrecv, gsend, grecv, s1, r1, s3, r3, s2, r2):
    n_lat, n_lon, _ = sizes
    lat, lon, dp = place()
    own, circle, channels = gu.shape
    f32, bf16 = jnp.float32, jnp.bfloat16
    loads = [
        pltpu.make_async_copy(src, dst, local.at[2 + k])
        for k, (src, dst) in enumerate(((w_hbm, weight), (wq_hbm, wq), (wo_hbm, wo)))
    ]
    for load in loads:
        load.start()
    one = sum_stages(sizes, big1, every1, a1, b1, c1, d1, e1, s1, r1)
    three = sum_stages(sizes, big3, every3, a3, b3, c3, d3, e3, s3, r3)
    two = sum_stages(sizes, big2, every2, a2, b2, c2, d2, e2, s2, r2)
    start_in, wait_fields, wait_cot, wait_sent = bring_rows(
        sizes, f_ref, c_ref, fp, cr, send, recv, xsend, xrecv, local
    )
    start_h, wait_h = halo_rows(sizes, gub, top, low, hsend, hrecv)
    start_r, wait_r = give_rows(n_lon, lon, result, result_out, rsend, rrecv)
    start_g, wait_g = give_rows(n_lon, lon, gf, gf_out, gsend, grecv)
    greet(sizes)
    start_in()
    loads[0].wait()
    wait_fields()
    pad[...] = fp[...].astype(f32).reshape(pad.shape)
    convolve(pad, weight, update, own, False)
    for load in loads[1:]:
        load.wait()
    steps = core_step(cr, update, gain_ref[...], wq, wo, result, gu, gub, big1, big3, go, gg)
    next(steps)
    start_r()
    wait_cot()
    next(steps)
    start_h()
    next(steps)
    one[0]()
    three[0]()
    next(steps)
    correlate_rows(pad, gu, conv, own)
    pack(big2, go, conv, gg)
    two[0]()
    one[1]()
    three[1]()
    wait_h()
    gpad[0:3] = top[...].astype(f32).reshape((3, circle, channels))
    gpad[3 : own + 3] = gu[...]
    gpad[own + 3 :] = low[...].astype(f32).reshape((3, circle, channels))
    convolve(gpad, weight, out, own, True)
    gf[...] = out[...].reshape(gf.shape).astype(bf16)
    two[1]()
    for k in range(2, len(one)):
        for stream in (one, three, two):
            stream[k]()
        if k == 3:
            start_g()
    wait_sent()
    wait_r()
    wait_g()


def on_device(sizes, fields, cotangent, conv_weight, norm_gain, w_qkv, w_out):
    n_lat, n_lon, n_dp = sizes
    batch, rows, cols, channels = fields.shape
    own, circle = rows // n_lon, cols * n_lon
    att = w_out.shape[0]
    bf16, f32 = jnp.bfloat16, jnp.float32
    shape = jax.ShapeDtypeStruct
    sems = pltpu.SemaphoreType.DMA
    vmem = pltpu.VMEM
    parts = n_lat * n_lon * n_dp
    part_rows = channels // parts
    widths = (w_qkv.shape[1] // 2, w_qkv.shape[1] // 2, att + LANES)
    turns = 4 + 2 * n_lon
    blocked = (own, n_lon, cols, channels)
    flat = (own, circle, channels)
    padded = (own + 6, circle, channels)
    sums = []
    for w in widths:
        sums += [vmem((n, part_rows, w), bf16) for n in (parts, parts // 2, parts // 2, n_lon, n_lon, n_lon)]
    inside = pl.BlockSpec(memory_space=pltpu.VMEM)
    outside = pl.BlockSpec(memory_space=pl.ANY)
    result, grad_fields, one, three, two = pl.pallas_call(
        functools.partial(layer, sizes),
        out_shape=[shape((rows, cols, channels), bf16)] * 2
        + [shape((parts, part_rows, w), bf16) for w in widths],
        in_specs=[outside, outside, outside, inside, outside, outside],
        out_specs=[inside] * 5,
        scratch_shapes=[
            vmem((own + 6,) + blocked[1:], bf16), vmem(blocked, bf16), vmem(conv_weight.shape, f32),
            vmem(w_qkv.shape, bf16), vmem(w_out.shape, bf16),
            vmem(padded, f32), vmem(flat, f32), vmem(blocked, bf16), vmem(flat, f32), vmem(blocked, bf16),
            vmem(w_out.shape, f32), vmem((1, channels), f32),
            vmem((3,) + blocked[1:], bf16), vmem((3,) + blocked[1:], bf16),
            vmem(padded, f32), vmem(flat, f32), vmem(blocked, bf16), vmem(conv_weight.shape, f32),
        ] + sums + [
            sems((2, n_lon)), sems((2, n_lon)), sems((2,)), sems((2, n_lon)), sems((5,)),
            sems((2,)), sems((2,)),
            sems((n_lon,)), sems((n_lon,)), sems((n_lon,)), sems((n_lon,)),
            sems((turns,)), sems((turns,)), sems((turns,)), sems((turns,)), sems((turns,)), sems((turns,)),
        ],
        compiler_params=pltpu.CompilerParams(
            vmem_limit_bytes=67043328, collective_id=1, has_side_effects=True
        ),
    )(fields[0], cotangent[0], conv_weight, norm_gain.reshape(1, channels), w_qkv, w_out)
    outs = pl.pallas_call(
        finish,
        out_shape=[shape((rows, cols, channels), bf16)] * 2
        + [shape(w_qkv.shape, f32), shape(w_out.shape, f32), shape(conv_weight.shape, f32),
           shape((1, channels), f32)],
        in_specs=[inside] * 5,
        out_specs=[inside] * 6,
        compiler_params=pltpu.CompilerParams(vmem_limit_bytes=67043328),
    )(one, three, two, result, grad_fields)
    return outs[0][None], outs[1][None], outs[2], outs[3], outs[4], outs[5].reshape(channels)


def pick(mesh, *args):
    sizes = tuple(mesh.shape[a] for a in AXES)
    _, rows, cols, channels = args[0].shape
    att = args[5].shape[0]
    n_lat, n_lon, n_dp = sizes
    parts = n_lat * n_lon * n_dp
    fits = (
        args[0].shape[0] == 1 and n_lat == 2 and n_dp == 2 and n_lon == 4
        and rows % n_lon == 0 and rows // n_lon >= 3 and cols % 8 == 0
        and LANES % (cols * n_lon) == 0 and (rows // n_lon * cols * n_lon) % LANES == 0
        and channels == 2 * att and channels % (8 * parts) == 0 and 64 % (channels // parts) == 0
        and att % LANES == 0 and args[4].shape[1] == 3 * att and 3 * att % (2 * LANES) == 0
    )
    return on_device(sizes, *args) if fits else on_device_native(*args)


def solution(mesh):
    placed = (
        P(("member", "dp"), "lat", "lon", None),
        P(("member", "dp"), "lat", "lon", None),
        P(),
        P(),
        P(),
        P(),
    )
    return jax.shard_map(
        functools.partial(pick, mesh),
        mesh=mesh,
        in_specs=placed,
        out_specs=(
            P(("member", "dp"), "lat", "lon", None),
            P(("member", "dp"), "lat", "lon", None),
            P("member", None),
            P("member", None),
            P("member", None, None),
            P("member"),
        ),
        check_vma=False,
    )
```
